128 devices in a mesh: pole: 8 (over z, core), lat: 16 (over x, y).
Axes of the slice: x: 4, y: 4, z: 4, core: 2. Of those that a mesh axis runs over, the one named last changes fastest.
Arguments:
- fields: bfloat16 [8, 3, 1280, 2560], P(None, None, ('pole', 'lat')), may hold values from -6 to 6
- cycle_weights: float32 [1280], P(('pole', 'lat')), may hold values from 0.5 to 2
- legendre: bfloat16 [1280, 640, 1281], P(None, ('pole', 'lat')), may hold values from -0.15625 to 0.15625
- inverses: float32 [2, 8, 640, 2, 3, 3, 1281], P(None, None, ('pole', 'lat')), may hold values from -0.4 to 1
- pole_coeffs: float32 [2, 2], replicated, may hold values from -3 to 3
- pair_order: int32 [640], replicated, may hold values from 0 to 639, each once
Outputs:
- result: float32 [8, 3, 1280, 2560], P(None, None, ('pole', 'lat'))
The draws below stay inside these ranges and needn't reach their ends.
Inputs may be any that keep to these rules, and one draw needn't show every extreme that they name: `pair_order`: each pair index appears once.
All inputs are finite; a program needn't handle non-finite values.
Results may differ from the reference program's by a relative error of at most 0.015.
Values may be sent and summed in bfloat16 or wider, within the bound.
No kernel may reach another device: no remote copies, remote signals or barrier semaphores. Data moves between devices by JAX's collectives and lax.ppermute only.
A program may use at most 192 MiB of HBM per device.

```python
import math
import jax
import jax.numpy as jnp
from jax import lax

NM = 1280
NLAT = 1280
NLON = 2560
FIELDS = 3
MODES = 8
POLES = 2
ITERS = 3
PAIRS = 640
NN = 1281


def draw_inverses(key, part):
    full_shape = (POLES, MODES, PAIRS, 2, 3, 3, NM + 1)
    uniform_base = jax.random.uniform(key, full_shape, jnp.float32)
    diag_mask = jnp.eye(3, dtype=jnp.float32).reshape(1, 1, 1, 1, 3, 3, 1)
    is_real = (jnp.arange(2) == 0).astype(jnp.float32).reshape(1, 1, 1, 2, 1, 1, 1)
    diag_values = is_real * (0.4 + 0.6 * uniform_base) + (1.0 - is_real) * (-0.4 + 0.8 * uniform_base)
    off_values = -0.25 + 0.5 * uniform_base
    return diag_mask * diag_values + (1.0 - diag_mask) * off_values


def block_scale(rng, extent, split, smallest, largest):
    gain, own = 1.0, jax.random.fold_in(rng, 6)
    for axis_at, blocks in split:
        steps = jnp.exp(jax.random.uniform(jax.random.fold_in(own, axis_at), (blocks,), jnp.float32, smallest / len(split), largest / len(split)))
        gain = gain * jnp.repeat(steps, extent[axis_at] // blocks).reshape([-1 if axis == axis_at else 1 for axis in range(len(extent))])
    return gain


def bell_draw(own_key, extent, width, bound, split=(), held_as=jnp.bfloat16):
    level = block_scale(own_key, extent, split, -0.22, 0.18) if split else 1.0
    array = jax.random.normal(own_key, extent, jnp.float32) * width * level
    return jnp.minimum(jnp.maximum(array, -bound), bound).astype(held_as)


def setup_inputs(seed: int = 0) -> dict:
    seeds = jax.random.split(jax.random.key(seed), 7)
    return {
        "fields": bell_draw(seeds[0], (MODES, FIELDS, NLAT, NLON), 1.0, 6.0, ((2, 128),)),
        "cycle_weights": jnp.clip(jnp.exp(math.log(2.0) - 1.3862944 * jax.random.uniform(seeds[1], (NLAT,), jnp.float32) ** block_scale(seeds[1], (NLAT,), ((0, 128),), -0.2, 0.2)), 0.5, 2.0),
        "legendre": bell_draw(seeds[2], (NLAT, PAIRS, NN), NM ** -0.5, 0.15625, ((1, 128),)),
        "inverses": draw_inverses(jax.random.fold_in(seeds[6], 71), 0),
        "pole_coeffs": bell_draw(seeds[4], (POLES, 2), 0.5, 3.0, (), jnp.float32),
        "pair_order": jax.random.permutation(seeds[5], PAIRS).astype(jnp.int32),
    }


ROTATION = 0.4
PRECISE = lax.Precision.HIGHEST

def coupling_weights(first_pair, wave_count, length):
    offset = jnp.arange(length, dtype=jnp.int32)
    base_pair = first_pair[..., None]
    in_first = offset < wave_count - base_pair
    order_int = jnp.where(in_first, base_pair, wave_count - 1 - base_pair)
    degree = jnp.where(in_first, base_pair + offset, offset - 1)
    order_m = order_int.astype(jnp.float32)
    lower_n = degree.astype(jnp.float32)
    upper_n = lower_n + 1.0
    down_ratio = jnp.maximum(lower_n * lower_n - order_m * order_m, 0.0) / jnp.maximum(4.0 * lower_n * lower_n - 1.0, 1.0)
    up_ratio = jnp.maximum(upper_n * upper_n - order_m * order_m, 0.0) / (4.0 * upper_n * upper_n - 1.0)
    eps_down = jnp.where(degree > order_int, ROTATION * jnp.sqrt(down_ratio), 0.0)
    eps_up = jnp.where(degree + 1 < wave_count, ROTATION * jnp.sqrt(up_ratio), 0.0)
    return (in_first, eps_down, eps_up)

def shift_prev(values):
    return jnp.concatenate([jnp.zeros_like(values[..., :1]), values[..., :-1]], axis=-1)

def shift_next(values):
    return jnp.concatenate([values[..., 1:], jnp.zeros_like(values[..., :1])], axis=-1)

def couple_fields(current, eps_down, eps_up):
    diverge = current[:, :, 1]
    vortic = current[:, :, 2]
    to_div = eps_down * shift_prev(vortic) + eps_up * shift_next(vortic)
    to_vort = eps_down * shift_prev(diverge) + eps_up * shift_next(diverge)
    return jnp.stack([jnp.zeros_like(to_div), to_div, to_vort], axis=2)

def reference(fields, cycle_weights, legendre, inverses, pole_coeffs, pair_order):
    wave_count = NM
    column_span = NM + 1
    spectrum = jnp.fft.rfft(fields.astype(jnp.float32), axis=-1)[..., :wave_count] / math.sqrt(NLON)
    coeff_real = jnp.real(spectrum).astype(jnp.float32)
    coeff_imag = jnp.imag(spectrum).astype(jnp.float32)
    stacked = jnp.stack([coeff_real, coeff_imag], axis=2)
    weighted = lax.optimization_barrier((stacked * cycle_weights[:, None]).astype(jnp.bfloat16))
    beta_real = pole_coeffs[:, 0].reshape(-1, 1, 1, 1)
    beta_imag = pole_coeffs[:, 1].reshape(-1, 1, 1, 1)

    def per_slot(slot_index):
        first_pair = pair_order[slot_index]
        leg_table = lax.dynamic_index_in_dim(legendre, slot_index, 1, keepdims=False).astype(jnp.float32)
        column_a = lax.dynamic_index_in_dim(weighted, first_pair, 4, keepdims=False).astype(jnp.float32)
        column_b = lax.dynamic_index_in_dim(weighted, wave_count - 1 - first_pair, 4, keepdims=False).astype(jnp.float32)
        in_first, eps_down, eps_up = coupling_weights(first_pair, wave_count, column_span)
        spec_a = jnp.einsum('mfrl,lk->mfrk', column_a, leg_table, precision=PRECISE)
        spec_b = jnp.einsum('mfrl,lk->mfrk', column_b, leg_table, precision=PRECISE)
        spectral = jnp.where(in_first, spec_a, spec_b)
        blocks = lax.dynamic_index_in_dim(inverses, slot_index, 2, keepdims=False)
        inv_real = blocks[:, :, 0]
        inv_imag = blocks[:, :, 1]

        def apply_blocks(part_real, part_imag):
            first_term = jnp.einsum('pmick,pmck->pmik', inv_real, part_real, precision=PRECISE)
            second_term = jnp.einsum('pmick,pmck->pmik', inv_imag, part_imag, precision=PRECISE)
            third_term = jnp.einsum('pmick,pmck->pmik', inv_real, part_imag, precision=PRECISE)
            fourth_term = jnp.einsum('pmick,pmck->pmik', inv_imag, part_real, precision=PRECISE)
            return (first_term - second_term, third_term + fourth_term)
        rhs_real = jnp.broadcast_to(spectral[:, :, 0][None], (POLES,) + spectral[:, :, 0].shape)
        rhs_imag = jnp.broadcast_to(spectral[:, :, 1][None], (POLES,) + spectral[:, :, 1].shape)
        sol_real, sol_imag = apply_blocks(rhs_real, rhs_imag)
        for repeat in range(ITERS):
            sol_real, sol_imag = apply_blocks(rhs_real - couple_fields(sol_real, eps_down, eps_up), rhs_imag - couple_fields(sol_imag, eps_down, eps_up))
        comb_real = lax.optimization_barrier(jnp.sum(beta_real * sol_real - beta_imag * sol_imag, axis=0))
        comb_imag = lax.optimization_barrier(jnp.sum(beta_real * sol_imag + beta_imag * sol_real, axis=0))
        rounded = lax.optimization_barrier(jnp.stack([comb_real, comb_imag], axis=2).astype(jnp.bfloat16))
        combined = rounded.astype(jnp.float32)
        syn_a = jnp.einsum('mfrk,lk->mfrl', jnp.where(in_first, combined, 0.0), leg_table, precision=PRECISE).astype(jnp.bfloat16)
        syn_b = jnp.einsum('mfrk,lk->mfrl', jnp.where(in_first, 0.0, combined), leg_table, precision=PRECISE).astype(jnp.bfloat16)
        return (syn_a, syn_b)
    syn_a, syn_b = lax.map(per_slot, jnp.arange(PAIRS, dtype=jnp.int32))
    by_pair_a = jnp.zeros_like(syn_a).at[pair_order].set(syn_a)
    by_pair_b = jnp.zeros_like(syn_b).at[pair_order].set(syn_b)
    part_low = jnp.moveaxis(by_pair_a, 0, -1)
    part_high = jnp.flip(jnp.moveaxis(by_pair_b, 0, -1), axis=-1)
    coeffs = jnp.concatenate([part_low, part_high], axis=-1).astype(jnp.float32)
    padding = ((0, 0), (0, 0), (0, 0), (0, NLON // 2 + 1 - wave_count))
    full_real = jnp.pad(coeffs[:, :, 0], padding)
    full_imag = jnp.pad(coeffs[:, :, 1], padding)
    grid_out = jnp.fft.irfft(full_real + 1j * full_imag, n=NLON, axis=-1) * math.sqrt(NLON)
    return grid_out.astype(jnp.float32)
```

```python
import functools
import math

import jax
import jax.numpy as jnp
from jax import lax
from jax.experimental import pallas as pl
from jax.experimental.pallas import tpu as pltpu
from jax.sharding import PartitionSpec as P

ITERS = 3
ROTATION = 0.4
AXES = ("pole", "lat")
F32 = jnp.float32
BF16 = jnp.bfloat16
NT = (((1,), (1,)), ((), ()))
NN = (((1,), (0,)), ((), ()))

MODES, FIELDS, CYCLES, LONS = 8, 3, 10, 2560
DEVS, SLOTS, WAVES = 128, 5, 1280
HALF = LONS // 2
NLAT = DEVS * CYCLES
COLS = WAVES + 1
WIDE = 1408
HALF_CYCLES = CYCLES // 2
ROWS = 40
LANES = 128


def sin_cos(product):
    turns = jnp.floor(product * (4.0 / LONS) + 0.5)
    angle = (product - turns * (LONS / 4.0)) * (2.0 * math.pi / LONS)
    z = angle * angle
    s = angle * (1.0 + z * (-1.0 / 6 + z * (1.0 / 120 + z * (-1.0 / 5040))))
    c = 1.0 + z * (-0.5 + z * (1.0 / 24 + z * (-1.0 / 720 + z * (1.0 / 40320))))
    quarter = turns.astype(jnp.int32) & 3
    swap = (quarter & 1) == 1
    sine = jnp.where(swap, c, s)
    cosine = jnp.where(swap, s, c)
    sine = jnp.where(quarter >= 2, -sine, sine)
    cosine = jnp.where((quarter == 1) | (quarter == 2), -cosine, cosine)
    return sine, cosine


def forward_kernel(weight_ref, wave_ref, field_ref, table_ref, send_ref, grid_scr, pack_scr):
    slot = pl.program_id(0)

    @pl.when(slot == 0)
    def _():
        for half in range(2):
            for field in range(FIELDS):
                for c in range(HALF_CYCLES):
                    cycle = half * HALF_CYCLES + c
                    weight = weight_ref[cycle]
                    row = half * LANES + (field * HALF_CYCLES + c) * MODES
                    near = field_ref[field, cycle, :, :HALF].astype(F32) * weight
                    far = field_ref[field, cycle, :, HALF:].astype(F32) * weight
                    grid_scr[0, row : row + MODES, :] = (near + far).astype(BF16)
                    grid_scr[1, row : row + MODES, :] = (near - far).astype(BF16)
            row = half * LANES + FIELDS * HALF_CYCLES * MODES
            grid_scr[:, row : (half + 1) * LANES, :] = jnp.zeros((2, MODES, HALF), BF16)

    lane = lax.broadcasted_iota(jnp.int32, (32, LANES), 1).astype(F32)
    scale = 1.0 / math.sqrt(LONS)
    for parity in range(2):
        for chunk in range(4):
            wave = wave_ref[parity, 0, chunk * 32 : (chunk + 1) * 32, :]
            step_sin, step_cos = sin_cos(wave * float(LANES))
            sine, cosine = sin_cos(wave * lane)
            sine, cosine = sine * scale, cosine * scale
            for block in range(HALF // LANES):
                at = slice(block * LANES, (block + 1) * LANES)
                table_ref[parity, chunk * 32 : (chunk + 1) * 32, at] = cosine.astype(BF16)
                table_ref[parity, LANES + chunk * 32 : LANES + (chunk + 1) * 32, at] = (-sine).astype(BF16)
                sine, cosine = (
                    sine * step_cos + cosine * step_sin,
                    cosine * step_cos - sine * step_sin,
                )
        coeffs = lax.dot_general(table_ref[parity], grid_scr[parity], NT, preferred_element_type=F32)
        for part in range(2):
            for half in range(2):
                row = ((slot * 2 + parity) * 2 + part) * 2 + half
                pack_scr[pl.ds(row, DEVS, stride=ROWS), :] = coeffs[
                    part * LANES : (part + 1) * LANES, half * LANES : (half + 1) * LANES
                ]

    @pl.when(slot == SLOTS - 1)
    def _():
        send_ref[...] = pack_scr[...].astype(BF16)


def shift_prev(v):
    return pltpu.roll(v, 1, axis=1)


def shift_next(v):
    return pltpu.roll(v, WIDE - 1, axis=1)


def coupling_weights(pair):
    offset = lax.broadcasted_iota(jnp.int32, (MODES, WIDE), 1)
    in_first = offset < WAVES - pair
    order_int = jnp.where(in_first, pair, WAVES - 1 - pair)
    degree = jnp.where(in_first, pair + offset, offset - 1)
    order_m = order_int.astype(F32)
    lower_n = degree.astype(F32)
    upper_n = lower_n + 1.0
    down_ratio = jnp.maximum(lower_n * lower_n - order_m * order_m, 0.0) / jnp.maximum(
        4.0 * lower_n * lower_n - 1.0, 1.0
    )
    up_ratio = jnp.maximum(upper_n * upper_n - order_m * order_m, 0.0) / (
        4.0 * upper_n * upper_n - 1.0
    )
    real = offset < COLS
    eps_down = jnp.where((degree > order_int) & real, ROTATION * jnp.sqrt(down_ratio), 0.0)
    eps_up = jnp.where((degree + 1 < WAVES) & real, ROTATION * jnp.sqrt(up_ratio), 0.0)
    return in_first, eps_down, eps_up


def middle_kernel(
    owner_ref, pair_ref, pole_ref, recv_ref, order_ref, leg_ref, inv_ref, send_ref,
    pack_scr, cycle_scr, column_scr,
):
    slot = pl.program_id(0)

    @pl.when(slot == 0)
    def _():
        pack_scr[...] = recv_ref[...].astype(F32)
        for group in range(2 * SLOTS):
            turned = [
                jnp.transpose(pack_scr[pl.ds(group * 4 + row, DEVS, stride=ROWS), :])
                for row in range(4)
            ]
            for half in range(2):
                for c in range(HALF_CYCLES):
                    pieces = [
                        turned[part * 2 + half][
                            (field * HALF_CYCLES + c) * MODES : (field * HALF_CYCLES + c + 1) * MODES
                        ]
                        for part in range(2)
                        for field in range(FIELDS)
                    ]
                    at = (half * HALF_CYCLES + c) * LANES
                    cycle_scr[group * 48 : (group + 1) * 48, at : at + LANES] = jnp.concatenate(
                        pieces, axis=0
                    ).astype(BF16)
        column_scr[...] = lax.dot_general(
            cycle_scr[...], order_ref[...], NN, preferred_element_type=F32
        ).astype(BF16)

    pair = pair_ref[owner_ref[0] * SLOTS + slot]
    is_even = (pair & 1) == 0
    in_first, eps_down, eps_up = coupling_weights(pair)
    in_even = in_first == is_even
    rows = pl.ds(pl.multiple_of(slot * 96, 96), 96)
    column = column_scr[rows, :]
    spec = lax.dot_general(column, leg_ref[0, :WAVES, :], NT, preferred_element_type=F32)
    last = leg_ref[0, WAVES:COLS, :].astype(F32)
    spec_last = jnp.sum(column.astype(F32) * last, axis=1, keepdims=True)
    first_lane = lax.broadcasted_iota(jnp.int32, (96, LANES), 1) == 0
    spec = jnp.concatenate([spec, jnp.where(first_lane, spec_last, 0.0)], axis=1)
    rhs = [
        jnp.where(in_even, spec[g * MODES : (g + 1) * MODES], spec[48 + g * MODES : 48 + (g + 1) * MODES])
        for g in range(6)
    ]
    rhs = [(rhs[f], rhs[3 + f]) for f in range(FIELDS)]

    def couple(cur_real, cur_imag):
        return (
            eps_down * shift_prev(cur_real) + eps_up * shift_next(cur_real),
            eps_down * shift_prev(cur_imag) + eps_up * shift_next(cur_imag),
        )

    def apply(pole, row, terms):
        real, imag = None, None
        for c, (re, im) in terms:
            inv_re = inv_ref[0, pole, 0, row, c]
            inv_im = inv_ref[0, pole, 1, row, c]
            add_re = inv_re * re - inv_im * im
            add_im = inv_re * im + inv_im * re
            real = add_re if real is None else real + add_re
            imag = add_im if imag is None else imag + add_im
        return real, imag

    combined = [[None, None] for _ in range(FIELDS)]
    for pole in range(2):
        base = [apply(pole, f, list(enumerate(rhs))) for f in range(FIELDS)]
        div, vort = base[1], base[2]
        for step in range(ITERS):
            to_div, to_vort = couple(*vort), couple(*div)
            fields = range(FIELDS) if step == ITERS - 1 else (1, 2)
            solution = {}
            for f in fields:
                re, im = apply(pole, f, [(1, to_div), (2, to_vort)])
                solution[f] = (base[f][0] - re, base[f][1] - im)
            div, vort = solution[1], solution[2]
        beta_re = pole_ref[pole, 0]
        beta_im = pole_ref[pole, 1]
        for f in range(FIELDS):
            re, im = solution[f]
            add_re = beta_re * re - beta_im * im
            add_im = beta_re * im + beta_im * re
            combined[f][0] = add_re if pole == 0 else combined[f][0] + add_re
            combined[f][1] = add_im if pole == 0 else combined[f][1] + add_im

    groups = [combined[f][part] for part in range(2) for f in range(FIELDS)]
    even = jnp.concatenate([jnp.where(in_even, g, 0.0) for g in groups], axis=0)
    odd = jnp.concatenate([jnp.where(in_even, 0.0, g) for g in groups], axis=0)
    both = jnp.concatenate([even, odd], axis=0).astype(BF16)
    synth = lax.dot_general(both[:, :WAVES], leg_ref[0, :WAVES, :], NN, preferred_element_type=F32)
    synth = synth + both[:, WAVES : WAVES + 1].astype(F32) * last
    row_at = lax.broadcasted_iota(jnp.int32, (96, HALF), 0)
    synth = jnp.where((row_at < 48) & (pair == 0), synth, synth * 2.0)
    column_scr[rows, :] = synth.astype(BF16)

    @pl.when(slot == SLOTS - 1)
    def _():
        for group in range(2 * SLOTS):
            ordered = lax.dot_general(
                column_scr[group * 48 : (group + 1) * 48, :], order_ref[...], NT,
                preferred_element_type=F32,
            )
            for part in range(2):
                for half in range(2):
                    pieces = []
                    for field in range(FIELDS):
                        for c in range(HALF_CYCLES):
                            at = (half * HALF_CYCLES + c) * LANES
                            row = part * 24 + field * MODES
                            pieces.append(ordered[row : row + MODES, at : at + LANES])
                    pieces.append(jnp.zeros((MODES, LANES), F32))
                    turned = jnp.transpose(jnp.concatenate(pieces, axis=0))
                    pack_scr[pl.ds(group * 4 + part * 2 + half, DEVS, stride=ROWS), :] = turned
        send_ref[...] = pack_scr[...].astype(BF16)


def backward_kernel(recv_ref, table_ref, out_ref, pack_scr, wave_scr):
    step = pl.program_id(0)
    width = table_ref.shape[-1]

    @pl.when(step == 0)
    def _():
        pack_scr[...] = recv_ref[...].astype(F32)
        for slot in range(SLOTS):
            for parity in range(2):
                for part in range(2):
                    for half in range(2):
                        row = ((slot * 2 + parity) * 2 + part) * 2 + half
                        turned = jnp.transpose(pack_scr[pl.ds(row, DEVS, stride=ROWS), :])
                        at = (slot * 2 + part) * LANES
                        wave_scr[parity, half * LANES : (half + 1) * LANES, at : at + LANES] = turned.astype(BF16)

    even = lax.dot_general(wave_scr[0], table_ref[0], NN, preferred_element_type=F32)
    odd = lax.dot_general(wave_scr[1], table_ref[1], NN, preferred_element_type=F32)
    near = even + odd
    far = even - odd
    at = pl.multiple_of(step * width, width)
    for half in range(2):
        for field in range(FIELDS):
            for c in range(HALF_CYCLES):
                row = half * LANES + (field * HALF_CYCLES + c) * MODES
                cycle = half * HALF_CYCLES + c
                out_ref[field, cycle, :, pl.ds(at, width)] = near[row : row + MODES]
                out_ref[field, cycle, :, pl.ds(HALF + at, width)] = far[row : row + MODES]


def whole(shape):
    return pl.BlockSpec(shape, lambda i: (0,) * len(shape))


def on_device(fields, cycle_weights, legendre, inverses, pole_coeffs, pair_order):
    owner = lax.axis_index(AXES).astype(jnp.int32).reshape(1)
    smem = pl.BlockSpec(memory_space=pltpu.SMEM)
    grid_fields = jnp.transpose(fields, (1, 2, 0, 3))

    pairs = pair_order.reshape(DEVS, SLOTS).T
    is_even = (pairs & 1) == 0
    waves = jnp.stack([jnp.where(is_even, pairs, WAVES - 1 - pairs), jnp.where(is_even, WAVES - 1 - pairs, pairs)])
    waves = jnp.broadcast_to(waves.astype(F32)[..., None], (2, SLOTS, DEVS, LANES))

    table, outgoing = pl.pallas_call(
        forward_kernel,
        grid=(SLOTS,),
        in_specs=[
            smem,
            pl.BlockSpec((2, 1, DEVS, LANES), lambda i: (0, i, 0, 0)),
            whole((FIELDS, CYCLES, MODES, LONS)),
        ],
        out_specs=[
            pl.BlockSpec((2, 2 * DEVS, HALF), lambda i: (0, i, 0)),
            whole((DEVS * ROWS, LANES)),
        ],
        out_shape=[
            jax.ShapeDtypeStruct((2, HALF, HALF), BF16),
            jax.ShapeDtypeStruct((DEVS * ROWS, LANES), BF16),
        ],
        scratch_shapes=[
            pltpu.VMEM((2, 256, HALF), BF16),
            pltpu.VMEM((DEVS * ROWS, LANES), F32),
        ],
        name="forward",
    )(cycle_weights, waves, grid_fields)

    incoming = lax.all_to_all(
        outgoing.reshape(DEVS, ROWS, LANES), AXES, split_axis=0, concat_axis=0, tiled=True
    ).reshape(DEVS * ROWS, LANES)

    leg = jnp.transpose(legendre, (1, 2, 0))
    inv = jnp.transpose(inverses, (2, 0, 3, 4, 5, 1, 6))
    inv = jnp.pad(inv, ((0, 0),) * 6 + ((0, WIDE - COLS),))
    position = jnp.arange(NLAT, dtype=jnp.int32)
    natural = (position % DEVS) * CYCLES + position // DEVS
    order = (natural[:, None] == position[None, :]).astype(BF16)

    returning = pl.pallas_call(
        middle_kernel,
        grid=(SLOTS,),
        in_specs=[
            smem,
            smem,
            smem,
            whole((DEVS * ROWS, LANES)),
            whole((NLAT, NLAT)),
            pl.BlockSpec((1, COLS, NLAT), lambda i: (i, 0, 0)),
            pl.BlockSpec((1, 2, 2, 3, 3, MODES, WIDE), lambda i: (i, 0, 0, 0, 0, 0, 0)),
        ],
        out_specs=whole((DEVS * ROWS, LANES)),
        out_shape=jax.ShapeDtypeStruct((DEVS * ROWS, LANES), BF16),
        scratch_shapes=[
            pltpu.VMEM((DEVS * ROWS, LANES), F32),
            pltpu.VMEM((480, NLAT), BF16),
            pltpu.VMEM((480, NLAT), BF16),
        ],
        name="middle",
    )(owner, pair_order, pole_coeffs, incoming, order, leg, inv)

    back = lax.all_to_all(
        returning.reshape(DEVS, ROWS, LANES), AXES, split_axis=0, concat_axis=0, tiled=True
    ).reshape(DEVS * ROWS, LANES)

    width = 256
    result = pl.pallas_call(
        backward_kernel,
        grid=(HALF // width,),
        in_specs=[
            whole((DEVS * ROWS, LANES)),
            pl.BlockSpec((2, HALF, width), lambda i: (0, 0, i)),
        ],
        out_specs=whole((FIELDS, CYCLES, MODES, LONS)),
        out_shape=jax.ShapeDtypeStruct((FIELDS, CYCLES, MODES, LONS), F32),
        scratch_shapes=[
            pltpu.VMEM((DEVS * ROWS, LANES), F32),
            pltpu.VMEM((2, 256, HALF), BF16),
        ],
        name="backward",
    )(back, table)
    return jnp.transpose(result, (2, 0, 1, 3))


def solution(mesh):
    return jax.shard_map(
        on_device,
        mesh=mesh,
        in_specs=(
            P(None, None, AXES, None),
            P(AXES),
            P(None, AXES, None),
            P(None, None, AXES, None, None, None, None),
            P(),
            P(),
        ),
        out_specs=P(None, None, AXES, None),
        check_vma=False,
    )
```

```python
import functools
import math

import jax
import jax.numpy as jnp
from jax import lax
from jax.experimental import pallas as pl
from jax.experimental.pallas import tpu as pltpu
from jax.sharding import PartitionSpec as P

ITERS = 3
ROTATION = 0.4
AXES = ("pole", "lat")
F32 = jnp.float32
BF16 = jnp.bfloat16
NT = (((1,), (1,)), ((), ()))
NN = (((1,), (0,)), ((), ()))

MODES, FIELDS, CYCLES, LONS = 8, 3, 10, 2560
DEVS, SLOTS, WAVES = 128, 5, 1280
HALF = LONS // 2
NLAT = DEVS * CYCLES
COLS = WAVES + 1
WIDE = 1408
HALF_CYCLES = CYCLES // 2
ROWS = 40
LANES = 128
SUB = 8
GROUP = 24


def sin_cos(product):
    turns = jnp.floor(product * (4.0 / LONS) + 0.5)
    angle = (product - turns * (LONS / 4.0)) * (2.0 * math.pi / LONS)
    z = angle * angle
    s = angle * (1.0 + z * (-1.0 / 6 + z * (1.0 / 120 + z * (-1.0 / 5040))))
    c = 1.0 + z * (-0.5 + z * (1.0 / 24 + z * (-1.0 / 720 + z * (1.0 / 40320))))
    quarter = turns.astype(jnp.int32) & 3
    swap = (quarter & 1) == 1
    sine = jnp.where(swap, c, s)
    cosine = jnp.where(swap, s, c)
    sine = jnp.where(quarter >= 2, -sine, sine)
    cosine = jnp.where((quarter == 1) | (quarter == 2), -cosine, cosine)
    return sine, cosine


def forward_kernel(weight_ref, pair_ref, field_ref, table_ref, send_ref, grid_scr, pack_scr):
    slot = pl.program_id(0)

    @pl.when(slot == 0)
    def _():
        for half in range(2):
            for c in range(HALF_CYCLES):
                cycle = half * HALF_CYCLES + c
                weight = weight_ref[cycle]
                for field in range(FIELDS):
                    row = half * LANES + (c * FIELDS + field) * MODES
                    near = field_ref[field, cycle, :, :HALF].astype(F32) * weight
                    far = field_ref[field, cycle, :, HALF:].astype(F32) * weight
                    grid_scr[0, row : row + MODES, :] = (near + far).astype(BF16)
                    grid_scr[1, row : row + MODES, :] = (near - far).astype(BF16)
            row = half * LANES + FIELDS * HALF_CYCLES * MODES
            grid_scr[:, row : (half + 1) * LANES, :] = jnp.zeros((2, MODES, HALF), BF16)

    place = lax.broadcasted_iota(jnp.int32, (DEVS, LANES), 0) * SLOTS + slot
    source = jnp.zeros((DEVS, LANES), jnp.int32)
    for row in range(SLOTS):
        source = jnp.where(place >> 7 == row, pair_ref[row : row + 1, :], source)
    pair = jnp.take_along_axis(source, place & (LANES - 1), axis=1)
    is_even = (pair & 1) == 0
    waves = (jnp.where(is_even, pair, WAVES - 1 - pair), jnp.where(is_even, WAVES - 1 - pair, pair))

    lane = lax.broadcasted_iota(jnp.int32, (32, LANES), 1).astype(F32)
    scale = 1.0 / math.sqrt(LONS)
    for parity in range(2):
        for chunk in range(4):
            wave = waves[parity][chunk * 32 : (chunk + 1) * 32, :].astype(F32)
            step_sin, step_cos = sin_cos(wave * float(LANES))
            sine, cosine = sin_cos(wave * lane)
            sine, cosine = sine * scale, cosine * scale
            for block in range(HALF // LANES):
                at = slice(block * LANES, (block + 1) * LANES)
                table_ref[parity, chunk * 32 : (chunk + 1) * 32, at] = cosine.astype(BF16)
                table_ref[parity, LANES + chunk * 32 : LANES + (chunk + 1) * 32, at] = (-sine).astype(BF16)
                sine, cosine = (
                    sine * step_cos + cosine * step_sin,
                    cosine * step_cos - sine * step_sin,
                )
        coeffs = lax.dot_general(table_ref[parity], grid_scr[parity], NT, preferred_element_type=F32)
        for part in range(2):
            x = parity * 2 + part
            for half in range(2):
                piece = coeffs[part * LANES : (part + 1) * LANES, half * LANES : (half + 1) * LANES]
                if x:
                    piece = pltpu.roll(piece, GROUP * x, axis=1)
                pack_scr[pl.ds(x * 2 + half, DEVS, stride=SUB), :] = piece
    send_ref[...] = pack_scr[...].reshape(DEVS, SUB, LANES).astype(BF16)


def shift_prev(v):
    return pltpu.roll(v, 1, axis=1)


def shift_next(v):
    return pltpu.roll(v, WIDE - 1, axis=1)


def coupling_weights(pair):
    offset = lax.broadcasted_iota(jnp.int32, (MODES, WIDE), 1)
    in_first = offset < WAVES - pair
    order_int = jnp.where(in_first, pair, WAVES - 1 - pair)
    degree = jnp.where(in_first, pair + offset, offset - 1)
    order_m = order_int.astype(F32)
    lower_n = degree.astype(F32)
    upper_n = lower_n + 1.0
    down_ratio = jnp.maximum(lower_n * lower_n - order_m * order_m, 0.0) / jnp.maximum(
        4.0 * lower_n * lower_n - 1.0, 1.0
    )
    up_ratio = jnp.maximum(upper_n * upper_n - order_m * order_m, 0.0) / (
        4.0 * upper_n * upper_n - 1.0
    )
    real = offset < COLS
    eps_down = jnp.where((degree > order_int) & real, ROTATION * jnp.sqrt(down_ratio), 0.0)
    eps_up = jnp.where((degree + 1 < WAVES) & real, ROTATION * jnp.sqrt(up_ratio), 0.0)
    return in_first, eps_down, eps_up


def lane_group(position):
    lane = lax.broadcasted_iota(jnp.int32, (DEVS, LANES), 1)
    lane = lane - (GROUP * position) % LANES
    lane = jnp.where(lane < 0, lane + LANES, lane)
    return lane < GROUP


def middle_kernel(
    owner_ref, pair_ref, pole_ref, recv_ref, leg_ref, inv_ref, send_ref,
    pack_scr, cycle_scr, spec_scr, base,
):
    slot = base + pl.program_id(0)

    pack_scr[...] = recv_ref[...].astype(F32).reshape(DEVS * SUB, LANES)
    for half in range(2):
        rows = [pack_scr[pl.ds(x * 2 + half, DEVS, stride=SUB), :] for x in range(4)]
        for c in range(HALF_CYCLES):
            merged = rows[3]
            for x in range(3):
                merged = jnp.where(lane_group(c + x), rows[x], merged)
            if c:
                merged = pltpu.roll(merged, LANES - GROUP * c, axis=1)
            cycle_scr[pl.ds(half * HALF_CYCLES + c, DEVS, stride=CYCLES), :] = merged
    spec_scr[:COLS, :] = lax.dot_general(
        leg_ref[0], cycle_scr[...].astype(BF16), NN, preferred_element_type=F32
    )
    spec_scr[COLS:, :] = jnp.zeros((WIDE - COLS, LANES), F32)
    spec = jnp.concatenate(
        [jnp.transpose(spec_scr[t * LANES : (t + 1) * LANES, :])[:96] for t in range(WIDE // LANES)], axis=1
    )

    pair = pair_ref[owner_ref[0] * SLOTS + slot]
    is_even = (pair & 1) == 0
    in_first, eps_down, eps_up = coupling_weights(pair)
    in_even = in_first == is_even
    rhs = [
        jnp.where(in_even, spec[g * MODES : (g + 1) * MODES], spec[48 + g * MODES : 48 + (g + 1) * MODES])
        for g in range(6)
    ]
    rhs = [(rhs[f], rhs[3 + f]) for f in range(FIELDS)]

    def block(pole, part, row, c):
        values = inv_ref[0, pole, part, row, c]
        pad = jnp.zeros((MODES, WIDE - COLS), F32)
        return jnp.concatenate([values, pad], axis=1)

    def couple(cur_real, cur_imag):
        return (
            eps_down * shift_prev(cur_real) + eps_up * shift_next(cur_real),
            eps_down * shift_prev(cur_imag) + eps_up * shift_next(cur_imag),
        )

    def apply(pole, row, terms):
        real, imag = None, None
        for c, (re, im) in terms:
            inv_re = block(pole, 0, row, c)
            inv_im = block(pole, 1, row, c)
            add_re = inv_re * re - inv_im * im
            add_im = inv_re * im + inv_im * re
            real = add_re if real is None else real + add_re
            imag = add_im if imag is None else imag + add_im
        return real, imag

    combined = [[None, None] for _ in range(FIELDS)]
    for pole in range(2):
        base = [apply(pole, f, list(enumerate(rhs))) for f in range(FIELDS)]
        div, vort = base[1], base[2]
        for step in range(ITERS):
            to_div, to_vort = couple(*vort), couple(*div)
            fields = range(FIELDS) if step == ITERS - 1 else (1, 2)
            solution = {}
            for f in fields:
                re, im = apply(pole, f, [(1, to_div), (2, to_vort)])
                solution[f] = (base[f][0] - re, base[f][1] - im)
            div, vort = solution[1], solution[2]
        beta_re = pole_ref[pole, 0]
        beta_im = pole_ref[pole, 1]
        for f in range(FIELDS):
            re, im = solution[f]
            add_re = beta_re * re - beta_im * im
            add_im = beta_re * im + beta_im * re
            combined[f][0] = add_re if pole == 0 else combined[f][0] + add_re
            combined[f][1] = add_im if pole == 0 else combined[f][1] + add_im

    groups = [combined[f][part] for part in range(2) for f in range(FIELDS)]
    even = jnp.concatenate([jnp.where(in_even, g, 0.0) for g in groups], axis=0)
    odd = jnp.concatenate([jnp.where(in_even, 0.0, g) for g in groups], axis=0)
    both = jnp.concatenate([even, odd], axis=0).astype(BF16)
    synth = lax.dot_general(both[:, :WAVES], leg_ref[0, :WAVES, :], NN, preferred_element_type=F32)
    synth = synth + both[:, WAVES : WAVES + 1].astype(F32) * leg_ref[0, WAVES:COLS, :].astype(F32)
    row_at = lax.broadcasted_iota(jnp.int32, (96, NLAT), 0)
    synth = jnp.where((row_at < 48) & (pair == 0), synth, synth * 2.0)
    synth = jnp.concatenate([synth, jnp.zeros((32, NLAT), F32)], axis=0)
    for t in range(NLAT // LANES):
        cycle_scr[t * LANES : (t + 1) * LANES, :] = jnp.transpose(synth[:, t * LANES : (t + 1) * LANES])
    for half in range(2):
        turned = []
        for c in range(HALF_CYCLES):
            values = cycle_scr[pl.ds(half * HALF_CYCLES + c, DEVS, stride=CYCLES), :]
            turned.append(pltpu.roll(values, GROUP * c, axis=1) if c else values)
        for x in range(4):
            merged = turned[HALF_CYCLES - 1]
            for c in range(HALF_CYCLES - 1):
                merged = jnp.where(lane_group(c + x), turned[c], merged)
            pack_scr[pl.ds(x * 2 + half, DEVS, stride=SUB), :] = merged
    send_ref[...] = pack_scr[...].reshape(DEVS, SUB, LANES).astype(BF16)


def backward_kernel(recv_ref, table_ref, out_ref, pack_scr, wave_scr):
    step = pl.program_id(0)
    width = table_ref.shape[-1]

    @pl.when(step == 0)
    def _():
        pack_scr[...] = recv_ref[...].astype(F32).reshape(DEVS * ROWS, LANES)
        for slot in range(SLOTS):
            for x in range(4):
                parity, part = x // 2, x % 2
                at = (slot * 2 + part) * LANES
                for half in range(2):
                    row = slot * SUB + x * 2 + half
                    turned = jnp.transpose(pack_scr[pl.ds(row, DEVS, stride=ROWS), :])
                    if x:
                        turned = jnp.concatenate([turned[GROUP * x :], turned[: GROUP * x]], axis=0)
                    wave_scr[parity, half * LANES : (half + 1) * LANES, at : at + LANES] = turned.astype(BF16)

    even = lax.dot_general(wave_scr[0], table_ref[0], NN, preferred_element_type=F32)
    odd = lax.dot_general(wave_scr[1], table_ref[1], NN, preferred_element_type=F32)
    near = even + odd
    far = even - odd
    at = pl.multiple_of(step * width, width)
    for half in range(2):
        for c in range(HALF_CYCLES):
            for field in range(FIELDS):
                row = half * LANES + (c * FIELDS + field) * MODES
                cycle = half * HALF_CYCLES + c
                out_ref[field, cycle, :, pl.ds(at, width)] = near[row : row + MODES]
                out_ref[field, cycle, :, pl.ds(HALF + at, width)] = far[row : row + MODES]


def whole(shape):
    return pl.BlockSpec(shape, lambda i: (0,) * len(shape))


def exchange(messages):
    return lax.all_to_all(messages, AXES, split_axis=0, concat_axis=0, tiled=True)


def on_device(fields, cycle_weights, legendre, inverses, pole_coeffs, pair_order):
    owner = lax.axis_index(AXES).astype(jnp.int32).reshape(1)
    smem = pl.BlockSpec(memory_space=pltpu.SMEM)
    grid_fields = jnp.transpose(fields, (1, 2, 0, 3))

    table, outgoing = pl.pallas_call(
        forward_kernel,
        grid=(SLOTS,),
        in_specs=[
            smem,
            whole((SLOTS, LANES)),
            whole((FIELDS, CYCLES, MODES, LONS)),
        ],
        out_specs=[
            pl.BlockSpec((2, 2 * DEVS, HALF), lambda i: (0, i, 0)),
            pl.BlockSpec((DEVS, SUB, LANES), lambda i: (0, i, 0)),
        ],
        out_shape=[
            jax.ShapeDtypeStruct((2, HALF, HALF), BF16),
            jax.ShapeDtypeStruct((DEVS, ROWS, LANES), BF16),
        ],
        scratch_shapes=[
            pltpu.VMEM((2, 256, HALF), BF16),
            pltpu.VMEM((DEVS * SUB, LANES), F32),
        ],
        name="forward",
    )(cycle_weights, pair_order.reshape(SLOTS, LANES), grid_fields)

    incoming = exchange(outgoing)

    leg = jnp.transpose(legendre, (1, 2, 0))
    inv = jnp.transpose(inverses, (2, 0, 3, 4, 5, 1, 6))

    returning = pl.pallas_call(
        functools.partial(middle_kernel, base=0),
        grid=(SLOTS,),
        in_specs=[
            smem,
            smem,
            smem,
            pl.BlockSpec((DEVS, SUB, LANES), lambda i: (0, i, 0)),
            pl.BlockSpec((1, COLS, NLAT), lambda i: (i, 0, 0)),
            pl.BlockSpec((1, 2, 2, 3, 3, MODES, COLS), lambda i: (i, 0, 0, 0, 0, 0, 0)),
        ],
        out_specs=pl.BlockSpec((DEVS, SUB, LANES), lambda i: (0, i, 0)),
        out_shape=jax.ShapeDtypeStruct((DEVS, ROWS, LANES), BF16),
        scratch_shapes=[
            pltpu.VMEM((DEVS * SUB, LANES), F32),
            pltpu.VMEM((NLAT, LANES), F32),
            pltpu.VMEM((WIDE, LANES), F32),
        ],
        name="middle",
    )(owner, pair_order, pole_coeffs, incoming, leg, inv)

    back = exchange(returning)

    width = 256
    result = pl.pallas_call(
        backward_kernel,
        grid=(HALF // width,),
        in_specs=[
            whole((DEVS, ROWS, LANES)),
            pl.BlockSpec((2, HALF, width), lambda i: (0, 0, i)),
        ],
        out_specs=whole((FIELDS, CYCLES, MODES, LONS)),
        out_shape=jax.ShapeDtypeStruct((FIELDS, CYCLES, MODES, LONS), F32),
        scratch_shapes=[
            pltpu.VMEM((DEVS * ROWS, LANES), F32),
            pltpu.VMEM((2, 256, HALF), BF16),
        ],
        name="backward",
    )(back, table)
    return jnp.transpose(result, (2, 0, 1, 3))


def solution(mesh):
    return jax.shard_map(
        on_device,
        mesh=mesh,
        in_specs=(
            P(None, None, AXES, None),
            P(AXES),
            P(None, AXES, None),
            P(None, None, AXES, None, None, None, None),
            P(),
            P(),
        ),
        out_specs=P(None, None, AXES, None),
        check_vma=False,
    )
```

```python
import math

import jax
import jax.numpy as jnp
from jax import lax
from jax.experimental import pallas as pl
from jax.experimental.pallas import tpu as pltpu
from jax.sharding import PartitionSpec as P

ITERS = 3
ROTATION = 0.4
AXES = ("pole", "lat")
F32 = jnp.float32
BF16 = jnp.bfloat16
NT = (((1,), (1,)), ((), ()))
NN = (((1,), (0,)), ((), ()))

MODES, FIELDS, CYCLES, LONS = 8, 3, 10, 2560
DEVS, SLOTS, WAVES = 128, 5, 1280
HALF = LONS // 2
NLAT = DEVS * CYCLES
COLS = WAVES + 1
WIDE = 1408
HALF_CYCLES = CYCLES // 2
ROWS = 40
LANES = 128
SUB = 8
GROUP = 24


def sin_cos(product):
    turns = jnp.floor(product * (4.0 / LONS) + 0.5)
    angle = (product - turns * (LONS / 4.0)) * (2.0 * math.pi / LONS)
    z = angle * angle
    s = angle * (1.0 + z * (-1.0 / 6 + z * (1.0 / 120 + z * (-1.0 / 5040))))
    c = 1.0 + z * (-0.5 + z * (1.0 / 24 + z * (-1.0 / 720 + z * (1.0 / 40320))))
    quarter = turns.astype(jnp.int32) & 3
    swap = (quarter & 1) == 1
    sine = jnp.where(swap, c, s)
    cosine = jnp.where(swap, s, c)
    sine = jnp.where(quarter >= 2, -sine, sine)
    cosine = jnp.where((quarter == 1) | (quarter == 2), -cosine, cosine)
    return sine, cosine


def forward_kernel(weight_ref, pair_ref, field_ref, table_ref, send_ref, grid_scr, pack_scr):
    slot = pl.program_id(0)

    @pl.when(slot == 0)
    def _():
        for half in range(2):
            for c in range(HALF_CYCLES):
                cycle = half * HALF_CYCLES + c
                weight = weight_ref[cycle]
                for field in range(FIELDS):
                    row = half * LANES + (c * FIELDS + field) * MODES
                    near = field_ref[field, cycle, :, :HALF].astype(F32) * weight
                    far = field_ref[field, cycle, :, HALF:].astype(F32) * weight
                    grid_scr[0, row : row + MODES, :] = (near + far).astype(BF16)
                    grid_scr[1, row : row + MODES, :] = (near - far).astype(BF16)
            row = half * LANES + FIELDS * HALF_CYCLES * MODES
            grid_scr[:, row : (half + 1) * LANES, :] = jnp.zeros((2, MODES, HALF), BF16)

    place = lax.broadcasted_iota(jnp.int32, (DEVS, LANES), 0) * SLOTS + slot
    source = jnp.zeros((DEVS, LANES), jnp.int32)
    for row in range(SLOTS):
        source = jnp.where(place >> 7 == row, pair_ref[row : row + 1, :], source)
    pair = jnp.take_along_axis(source, place & (LANES - 1), axis=1)
    is_even = (pair & 1) == 0
    waves = (jnp.where(is_even, pair, WAVES - 1 - pair), jnp.where(is_even, WAVES - 1 - pair, pair))

    lane = lax.broadcasted_iota(jnp.int32, (32, LANES), 1).astype(F32)
    scale = 1.0 / math.sqrt(LONS)
    for parity in range(2):
        for chunk in range(4):
            wave = waves[parity][chunk * 32 : (chunk + 1) * 32, :].astype(F32)
            step_sin, step_cos = sin_cos(wave * float(LANES))
            sine, cosine = sin_cos(wave * lane)
            sine, cosine = sine * scale, cosine * scale
            for block in range(HALF // LANES):
                at = slice(block * LANES, (block + 1) * LANES)
                table_ref[parity, chunk * 32 : (chunk + 1) * 32, at] = cosine.astype(BF16)
                table_ref[parity, LANES + chunk * 32 : LANES + (chunk + 1) * 32, at] = (-sine).astype(BF16)
                sine, cosine = (
                    sine * step_cos + cosine * step_sin,
                    cosine * step_cos - sine * step_sin,
                )
        coeffs = lax.dot_general(table_ref[parity], grid_scr[parity], NT, preferred_element_type=F32)
        for part in range(2):
            x = parity * 2 + part
            for half in range(2):
                piece = coeffs[part * LANES : (part + 1) * LANES, half * LANES : (half + 1) * LANES]
                if x:
                    piece = pltpu.roll(piece, GROUP * x, axis=1)
                pack_scr[pl.ds(x * 2 + half, DEVS, stride=SUB), :] = piece
    send_ref[...] = pack_scr[...].reshape(DEVS, SUB, LANES).astype(BF16)


def shift_prev(v):
    return pltpu.roll(v, 1, axis=1)


def shift_next(v):
    return pltpu.roll(v, WIDE - 1, axis=1)


def coupling_weights(pair):
    offset = lax.broadcasted_iota(jnp.int32, (MODES, WIDE), 1)
    in_first = offset < WAVES - pair
    order_int = jnp.where(in_first, pair, WAVES - 1 - pair)
    degree = jnp.where(in_first, pair + offset, offset - 1)
    order_m = order_int.astype(F32)
    lower_n = degree.astype(F32)
    upper_n = lower_n + 1.0
    down_ratio = jnp.maximum(lower_n * lower_n - order_m * order_m, 0.0) / jnp.maximum(
        4.0 * lower_n * lower_n - 1.0, 1.0
    )
    up_ratio = jnp.maximum(upper_n * upper_n - order_m * order_m, 0.0) / (
        4.0 * upper_n * upper_n - 1.0
    )
    real = offset < COLS
    eps_down = jnp.where((degree > order_int) & real, ROTATION * jnp.sqrt(down_ratio), 0.0)
    eps_up = jnp.where((degree + 1 < WAVES) & real, ROTATION * jnp.sqrt(up_ratio), 0.0)
    return in_first, eps_down, eps_up


def lane_group(position):
    lane = lax.broadcasted_iota(jnp.int32, (DEVS, LANES), 1)
    lane = lane - (GROUP * position) % LANES
    lane = jnp.where(lane < 0, lane + LANES, lane)
    return lane < GROUP


def middle_kernel(
    owner_ref, pair_ref, pole_ref, recv_ref, leg_ref, inv_ref, send_ref,
    pack_scr, cycle_scr,
):
    slot = pl.program_id(0)

    pack_scr[...] = recv_ref[...].astype(F32).reshape(DEVS * SUB, LANES)
    for half in range(2):
        rows = [pack_scr[pl.ds(x * 2 + half, DEVS, stride=SUB), :] for x in range(4)]
        for c in range(HALF_CYCLES):
            merged = rows[3]
            for x in range(3):
                merged = jnp.where(lane_group(c + x), rows[x], merged)
            if c:
                merged = pltpu.roll(merged, LANES - GROUP * c, axis=1)
            cycle_scr[pl.ds(half * HALF_CYCLES + c, DEVS, stride=CYCLES), :] = merged
    column = jnp.concatenate(
        [jnp.transpose(cycle_scr[t * LANES : (t + 1) * LANES, :])[:96] for t in range(NLAT // LANES)], axis=1
    )
    last = leg_ref[0, WAVES:COLS, :].astype(F32)
    spec_last = jnp.sum(column * last, axis=1, keepdims=True)
    spec = lax.dot_general(column.astype(BF16), leg_ref[0, :WAVES, :], NT, preferred_element_type=F32)
    first_lane = lax.broadcasted_iota(jnp.int32, (96, LANES), 1) == 0
    spec = jnp.concatenate([spec, jnp.where(first_lane, spec_last, 0.0)], axis=1)

    pair = pair_ref[owner_ref[0] * SLOTS + slot]
    is_even = (pair & 1) == 0
    in_first, eps_down, eps_up = coupling_weights(pair)
    in_even = in_first == is_even
    rhs = [
        jnp.where(in_even, spec[g * MODES : (g + 1) * MODES], spec[48 + g * MODES : 48 + (g + 1) * MODES])
        for g in range(6)
    ]
    rhs = [(rhs[f], rhs[3 + f]) for f in range(FIELDS)]

    def couple(cur_real, cur_imag):
        return (
            eps_down * shift_prev(cur_real) + eps_up * shift_next(cur_real),
            eps_down * shift_prev(cur_imag) + eps_up * shift_next(cur_imag),
        )

    def apply(pole, row, terms):
        real, imag = None, None
        for c, (re, im) in terms:
            inv_re = inv_ref[0, pole, 0, row, c]
            inv_im = inv_ref[0, pole, 1, row, c]
            add_re = inv_re * re - inv_im * im
            add_im = inv_re * im + inv_im * re
            real = add_re if real is None else real + add_re
            imag = add_im if imag is None else imag + add_im
        return real, imag

    combined = [[None, None] for _ in range(FIELDS)]
    for pole in range(2):
        base = [apply(pole, f, list(enumerate(rhs))) for f in range(FIELDS)]
        div, vort = base[1], base[2]
        for step in range(ITERS):
            to_div, to_vort = couple(*vort), couple(*div)
            fields = range(FIELDS) if step == ITERS - 1 else (1, 2)
            solution = {}
            for f in fields:
                re, im = apply(pole, f, [(1, to_div), (2, to_vort)])
                solution[f] = (base[f][0] - re, base[f][1] - im)
            div, vort = solution[1], solution[2]
        beta_re = pole_ref[pole, 0]
        beta_im = pole_ref[pole, 1]
        for f in range(FIELDS):
            re, im = solution[f]
            add_re = beta_re * re - beta_im * im
            add_im = beta_re * im + beta_im * re
            combined[f][0] = add_re if pole == 0 else combined[f][0] + add_re
            combined[f][1] = add_im if pole == 0 else combined[f][1] + add_im

    groups = [combined[f][part] for part in range(2) for f in range(FIELDS)]
    even = jnp.concatenate([jnp.where(in_even, g, 0.0) for g in groups], axis=0)
    odd = jnp.concatenate([jnp.where(in_even, 0.0, g) for g in groups], axis=0)
    both = jnp.concatenate([even, odd], axis=0).astype(BF16)
    synth = lax.dot_general(both[:, :WAVES], leg_ref[0, :WAVES, :], NN, preferred_element_type=F32)
    synth = synth + both[:, WAVES : WAVES + 1].astype(F32) * last
    row_at = lax.broadcasted_iota(jnp.int32, (96, NLAT), 0)
    synth = jnp.where((row_at < 48) & (pair == 0), synth, synth * 2.0)
    synth = jnp.concatenate([synth, jnp.zeros((32, NLAT), F32)], axis=0)
    for t in range(NLAT // LANES):
        cycle_scr[t * LANES : (t + 1) * LANES, :] = jnp.transpose(synth[:, t * LANES : (t + 1) * LANES])
    for half in range(2):
        turned = []
        for c in range(HALF_CYCLES):
            values = cycle_scr[pl.ds(half * HALF_CYCLES + c, DEVS, stride=CYCLES), :]
            turned.append(pltpu.roll(values, GROUP * c, axis=1) if c else values)
        for x in range(4):
            merged = turned[HALF_CYCLES - 1]
            for c in range(HALF_CYCLES - 1):
                merged = jnp.where(lane_group(c + x), turned[c], merged)
            pack_scr[pl.ds(x * 2 + half, DEVS, stride=SUB), :] = merged
    send_ref[...] = pack_scr[...].reshape(DEVS, SUB, LANES).astype(BF16)


def backward_kernel(recv_ref, table_ref, out_ref, pack_scr, wave_scr):
    step = pl.program_id(0)
    width = table_ref.shape[-1]

    @pl.when(step == 0)
    def _():
        pack_scr[...] = recv_ref[...].astype(F32).reshape(DEVS * ROWS, LANES)
        for slot in range(SLOTS):
            for x in range(4):
                parity, part = x // 2, x % 2
                at = (slot * 2 + part) * LANES
                for half in range(2):
                    row = slot * SUB + x * 2 + half
                    turned = jnp.transpose(pack_scr[pl.ds(row, DEVS, stride=ROWS), :])
                    if x:
                        turned = jnp.concatenate([turned[GROUP * x :], turned[: GROUP * x]], axis=0)
                    wave_scr[parity, half * LANES : (half + 1) * LANES, at : at + LANES] = turned.astype(BF16)

    even = lax.dot_general(wave_scr[0], table_ref[0], NN, preferred_element_type=F32)
    odd = lax.dot_general(wave_scr[1], table_ref[1], NN, preferred_element_type=F32)
    near = even + odd
    far = even - odd
    at = pl.multiple_of(step * width, width)
    for half in range(2):
        for c in range(HALF_CYCLES):
            for field in range(FIELDS):
                row = half * LANES + (c * FIELDS + field) * MODES
                cycle = half * HALF_CYCLES + c
                out_ref[field, cycle, :, pl.ds(at, width)] = near[row : row + MODES]
                out_ref[field, cycle, :, pl.ds(HALF + at, width)] = far[row : row + MODES]


def whole(shape):
    return pl.BlockSpec(shape, lambda i: (0,) * len(shape))


def exchange(messages):
    return lax.all_to_all(messages, AXES, split_axis=0, concat_axis=0, tiled=True)


def on_device(fields, cycle_weights, legendre, inverses, pole_coeffs, pair_order):
    owner = lax.axis_index(AXES).astype(jnp.int32).reshape(1)
    smem = pl.BlockSpec(memory_space=pltpu.SMEM)
    grid_fields = jnp.transpose(fields, (1, 2, 0, 3))

    table, outgoing = pl.pallas_call(
        forward_kernel,
        grid=(SLOTS,),
        in_specs=[
            smem,
            whole((SLOTS, LANES)),
            whole((FIELDS, CYCLES, MODES, LONS)),
        ],
        out_specs=[
            pl.BlockSpec((2, 2 * DEVS, HALF), lambda i: (0, i, 0)),
            pl.BlockSpec((DEVS, SUB, LANES), lambda i: (0, i, 0)),
        ],
        out_shape=[
            jax.ShapeDtypeStruct((2, HALF, HALF), BF16),
            jax.ShapeDtypeStruct((DEVS, ROWS, LANES), BF16),
        ],
        scratch_shapes=[
            pltpu.VMEM((2, 256, HALF), BF16),
            pltpu.VMEM((DEVS * SUB, LANES), F32),
        ],
        name="forward",
    )(cycle_weights, pair_order.reshape(SLOTS, LANES), grid_fields)

    incoming = exchange(outgoing)

    leg = jnp.transpose(legendre, (1, 2, 0))
    inv = jnp.transpose(inverses, (2, 0, 3, 4, 5, 1, 6))
    inv = jnp.pad(inv, ((0, 0),) * 6 + ((0, WIDE - COLS),))

    returning = pl.pallas_call(
        middle_kernel,
        grid=(SLOTS,),
        in_specs=[
            smem,
            smem,
            smem,
            pl.BlockSpec((DEVS, SUB, LANES), lambda i: (0, i, 0)),
            pl.BlockSpec((1, COLS, NLAT), lambda i: (i, 0, 0)),
            pl.BlockSpec((1, 2, 2, 3, 3, MODES, WIDE), lambda i: (i, 0, 0, 0, 0, 0, 0)),
        ],
        out_specs=pl.BlockSpec((DEVS, SUB, LANES), lambda i: (0, i, 0)),
        out_shape=jax.ShapeDtypeStruct((DEVS, ROWS, LANES), BF16),
        scratch_shapes=[
            pltpu.VMEM((DEVS * SUB, LANES), F32),
            pltpu.VMEM((NLAT, LANES), F32),
        ],
        compiler_params=pltpu.CompilerParams(vmem_limit_bytes=32 << 20),
        name="middle",
    )(owner, pair_order, pole_coeffs, incoming, leg, inv)

    back = exchange(returning)

    width = 256
    result = pl.pallas_call(
        backward_kernel,
        grid=(HALF // width,),
        in_specs=[
            whole((DEVS, ROWS, LANES)),
            pl.BlockSpec((2, HALF, width), lambda i: (0, 0, i)),
        ],
        out_specs=whole((FIELDS, CYCLES, MODES, LONS)),
        out_shape=jax.ShapeDtypeStruct((FIELDS, CYCLES, MODES, LONS), F32),
        scratch_shapes=[
            pltpu.VMEM((DEVS * ROWS, LANES), F32),
            pltpu.VMEM((2, 256, HALF), BF16),
        ],
        name="backward",
    )(back, table)
    return jnp.transpose(result, (2, 0, 1, 3))


def solution(mesh):
    return jax.shard_map(
        on_device,
        mesh=mesh,
        in_specs=(
            P(None, None, AXES, None),
            P(AXES),
            P(None, AXES, None),
            P(None, None, AXES, None, None, None, None),
            P(),
            P(),
        ),
        out_specs=P(None, None, AXES, None),
        check_vma=False,
    )
```

```python
import math

import jax
import jax.numpy as jnp
from jax import lax
from jax.experimental import pallas as pl
from jax.experimental.pallas import tpu as pltpu
from jax.sharding import PartitionSpec as P

ITERS = 3
ROTATION = 0.4
AXES = ("pole", "lat")
F32 = jnp.float32
BF16 = jnp.bfloat16
NT = (((1,), (1,)), ((), ()))
NN = (((1,), (0,)), ((), ()))

MODES, FIELDS, CYCLES, LONS = 8, 3, 10, 2560
DEVS, SLOTS, WAVES = 128, 5, 1280
HALF = LONS // 2
NLAT = DEVS * CYCLES
COLS = WAVES + 1
WIDE = 1408
HALF_CYCLES = CYCLES // 2
ROWS = 40
LANES = 128
SUB = 8
GROUP = 24


def sin_cos(product):
    turns = jnp.floor(product * (4.0 / LONS) + 0.5)
    angle = (product - turns * (LONS / 4.0)) * (2.0 * math.pi / LONS)
    z = angle * angle
    s = angle * (1.0 + z * (-1.0 / 6 + z * (1.0 / 120 + z * (-1.0 / 5040))))
    c = 1.0 + z * (-0.5 + z * (1.0 / 24 + z * (-1.0 / 720 + z * (1.0 / 40320))))
    quarter = turns.astype(jnp.int32) & 3
    swap = (quarter & 1) == 1
    sine = jnp.where(swap, c, s)
    cosine = jnp.where(swap, s, c)
    sine = jnp.where(quarter >= 2, -sine, sine)
    cosine = jnp.where((quarter == 1) | (quarter == 2), -cosine, cosine)
    return sine, cosine


def forward_kernel(weight_ref, pair_ref, field_ref, table_ref, send_ref, grid_scr, pack_scr):
    slot = pl.program_id(0)

    @pl.when(slot == 0)
    def _():
        for half in range(2):
            for c in range(HALF_CYCLES):
                cycle = half * HALF_CYCLES + c
                weight = weight_ref[cycle]
                for field in range(FIELDS):
                    row = half * LANES + (c * FIELDS + field) * MODES
                    near = field_ref[field, cycle, :, :HALF].astype(F32) * weight
                    far = field_ref[field, cycle, :, HALF:].astype(F32) * weight
                    grid_scr[0, row : row + MODES, :] = (near + far).astype(BF16)
                    grid_scr[1, row : row + MODES, :] = (near - far).astype(BF16)
            row = half * LANES + FIELDS * HALF_CYCLES * MODES
            grid_scr[:, row : (half + 1) * LANES, :] = jnp.zeros((2, MODES, HALF), BF16)

    place = lax.broadcasted_iota(jnp.int32, (DEVS, LANES), 0) * SLOTS + slot
    source = jnp.zeros((DEVS, LANES), jnp.int32)
    for row in range(SLOTS):
        source = jnp.where(place >> 7 == row, pair_ref[row : row + 1, :], source)
    pair = jnp.take_along_axis(source, place & (LANES - 1), axis=1)
    is_even = (pair & 1) == 0
    waves = (jnp.where(is_even, pair, WAVES - 1 - pair), jnp.where(is_even, WAVES - 1 - pair, pair))

    lane = lax.broadcasted_iota(jnp.int32, (32, LANES), 1).astype(F32)
    scale = 1.0 / math.sqrt(LONS)
    for parity in range(2):
        for chunk in range(4):
            wave = waves[parity][chunk * 32 : (chunk + 1) * 32, :].astype(F32)
            step_sin, step_cos = sin_cos(wave * float(LANES))
            sine, cosine = sin_cos(wave * lane)
            sine, cosine = sine * scale, cosine * scale
            for block in range(HALF // LANES):
                at = slice(block * LANES, (block + 1) * LANES)
                table_ref[parity, chunk * 32 : (chunk + 1) * 32, at] = cosine.astype(BF16)
                table_ref[parity, LANES + chunk * 32 : LANES + (chunk + 1) * 32, at] = (-sine).astype(BF16)
                sine, cosine = (
                    sine * step_cos + cosine * step_sin,
                    cosine * step_cos - sine * step_sin,
                )
        coeffs = lax.dot_general(table_ref[parity], grid_scr[parity], NT, preferred_element_type=F32)
        for part in range(2):
            x = parity * 2 + part
            for half in range(2):
                piece = coeffs[part * LANES : (part + 1) * LANES, half * LANES : (half + 1) * LANES]
                if x:
                    piece = pltpu.roll(piece, GROUP * x, axis=1)
                pack_scr[pl.ds(x * 2 + half, DEVS, stride=SUB), :] = piece
    send_ref[...] = pack_scr[...].reshape(DEVS, SUB, LANES).astype(BF16)


def shift_prev(v):
    return pltpu.roll(v, 1, axis=1)


def shift_next(v):
    return pltpu.roll(v, WIDE - 1, axis=1)


def coupling_weights(pair):
    offset = lax.broadcasted_iota(jnp.int32, (MODES, WIDE), 1)
    in_first = offset < WAVES - pair
    order_int = jnp.where(in_first, pair, WAVES - 1 - pair)
    degree = jnp.where(in_first, pair + offset, offset - 1)
    order_m = order_int.astype(F32)
    lower_n = degree.astype(F32)
    upper_n = lower_n + 1.0
    down_ratio = jnp.maximum(lower_n * lower_n - order_m * order_m, 0.0) / jnp.maximum(
        4.0 * lower_n * lower_n - 1.0, 1.0
    )
    up_ratio = jnp.maximum(upper_n * upper_n - order_m * order_m, 0.0) / (
        4.0 * upper_n * upper_n - 1.0
    )
    real = offset < COLS
    eps_down = jnp.where((degree > order_int) & real, ROTATION * jnp.sqrt(down_ratio), 0.0)
    eps_up = jnp.where((degree + 1 < WAVES) & real, ROTATION * jnp.sqrt(up_ratio), 0.0)
    return in_first, eps_down, eps_up


def lane_group(position):
    lane = lax.broadcasted_iota(jnp.int32, (DEVS, LANES), 1)
    lane = lane - (GROUP * position) % LANES
    lane = jnp.where(lane < 0, lane + LANES, lane)
    return lane < GROUP


def middle_kernel(
    owner_ref, pair_ref, pole_ref, recv_ref, leg_ref, inv_ref, send_ref,
    pack_scr, cycle_scr,
):
    slot = pl.program_id(0)

    pack_scr[...] = recv_ref[...].astype(F32).reshape(DEVS * SUB, LANES)
    for half in range(2):
        rows = [pack_scr[pl.ds(x * 2 + half, DEVS, stride=SUB), :] for x in range(4)]
        for c in range(HALF_CYCLES):
            merged = rows[3]
            for x in range(3):
                merged = jnp.where(lane_group(c + x), rows[x], merged)
            if c:
                merged = pltpu.roll(merged, LANES - GROUP * c, axis=1)
            cycle_scr[pl.ds(half * HALF_CYCLES + c, DEVS, stride=CYCLES), :] = merged
    column = jnp.concatenate(
        [jnp.transpose(cycle_scr[t * LANES : (t + 1) * LANES, :])[:96] for t in range(NLAT // LANES)], axis=1
    )
    last = leg_ref[0, WAVES:COLS, :].astype(F32)
    spec_last = jnp.sum(column * last, axis=1, keepdims=True)
    spec = lax.dot_general(column.astype(BF16), leg_ref[0, :WAVES, :], NT, preferred_element_type=F32)
    first_lane = lax.broadcasted_iota(jnp.int32, (96, LANES), 1) == 0
    spec = jnp.concatenate([spec, jnp.where(first_lane, spec_last, 0.0)], axis=1)

    pair = pair_ref[owner_ref[0] * SLOTS + slot]
    is_even = (pair & 1) == 0
    in_first, eps_down, eps_up = coupling_weights(pair)
    in_even = in_first == is_even
    rhs = [
        jnp.where(in_even, spec[g * MODES : (g + 1) * MODES], spec[48 + g * MODES : 48 + (g + 1) * MODES])
        for g in range(6)
    ]
    rhs = [(rhs[f], rhs[3 + f]) for f in range(FIELDS)]

    def couple(cur_real, cur_imag):
        return (
            eps_down * shift_prev(cur_real) + eps_up * shift_next(cur_real),
            eps_down * shift_prev(cur_imag) + eps_up * shift_next(cur_imag),
        )

    def apply(pole, row, terms):
        real, imag = None, None
        for c, (re, im) in terms:
            inv_re = inv_ref[0, pole, 0, row, c]
            inv_im = inv_ref[0, pole, 1, row, c]
            add_re = inv_re * re - inv_im * im
            add_im = inv_re * im + inv_im * re
            real = add_re if real is None else real + add_re
            imag = add_im if imag is None else imag + add_im
        return real, imag

    combined = [[None, None] for _ in range(FIELDS)]
    for pole in range(2):
        base = [apply(pole, f, list(enumerate(rhs))) for f in range(FIELDS)]
        div, vort = base[1], base[2]
        for step in range(ITERS):
            to_div, to_vort = couple(*vort), couple(*div)
            fields = range(FIELDS) if step == ITERS - 1 else (1, 2)
            solution = {}
            for f in fields:
                re, im = apply(pole, f, [(1, to_div), (2, to_vort)])
                solution[f] = (base[f][0] - re, base[f][1] - im)
            div, vort = solution[1], solution[2]
        beta_re = pole_ref[pole, 0]
        beta_im = pole_ref[pole, 1]
        for f in range(FIELDS):
            re, im = solution[f]
            add_re = beta_re * re - beta_im * im
            add_im = beta_re * im + beta_im * re
            combined[f][0] = add_re if pole == 0 else combined[f][0] + add_re
            combined[f][1] = add_im if pole == 0 else combined[f][1] + add_im

    groups = [combined[f][part] for part in range(2) for f in range(FIELDS)]
    even = jnp.concatenate([jnp.where(in_even, g, 0.0) for g in groups], axis=0)
    odd = jnp.concatenate([jnp.where(in_even, 0.0, g) for g in groups], axis=0)
    both = jnp.concatenate([even, odd], axis=0).astype(BF16)
    synth = lax.dot_general(both[:, :WAVES], leg_ref[0, :WAVES, :], NN, preferred_element_type=F32)
    synth = synth + both[:, WAVES : WAVES + 1].astype(F32) * last
    row_at = lax.broadcasted_iota(jnp.int32, (96, NLAT), 0)
    synth = jnp.where((row_at < 48) & (pair == 0), synth, synth * 2.0)
    synth = jnp.concatenate([synth, jnp.zeros((32, NLAT), F32)], axis=0)
    for t in range(NLAT // LANES):
        cycle_scr[t * LANES : (t + 1) * LANES, :] = jnp.transpose(synth[:, t * LANES : (t + 1) * LANES])
    for half in range(2):
        turned = []
        for c in range(HALF_CYCLES):
            values = cycle_scr[pl.ds(half * HALF_CYCLES + c, DEVS, stride=CYCLES), :]
            turned.append(pltpu.roll(values, GROUP * c, axis=1) if c else values)
        for x in range(4):
            merged = turned[HALF_CYCLES - 1]
            for c in range(HALF_CYCLES - 1):
                merged = jnp.where(lane_group(c + x), turned[c], merged)
            pack_scr[pl.ds(x * 2 + half, DEVS, stride=SUB), :] = merged
    send_ref[...] = pack_scr[...].reshape(DEVS, SUB, LANES).astype(BF16)


def backward_kernel(recv_ref, table_ref, out_ref, pack_scr, wave_scr):
    step = pl.program_id(0)
    width = table_ref.shape[-1]

    @pl.when(step == 0)
    def _():
        pack_scr[...] = recv_ref[...].astype(F32).reshape(DEVS * ROWS, LANES)
        for slot in range(SLOTS):
            for x in range(4):
                parity, part = x // 2, x % 2
                at = (slot * 2 + part) * LANES
                for half in range(2):
                    row = slot * SUB + x * 2 + half
                    turned = jnp.transpose(pack_scr[pl.ds(row, DEVS, stride=ROWS), :])
                    if x:
                        turned = jnp.concatenate([turned[GROUP * x :], turned[: GROUP * x]], axis=0)
                    wave_scr[parity, half * LANES : (half + 1) * LANES, at : at + LANES] = turned.astype(BF16)

    even = lax.dot_general(wave_scr[0], table_ref[0], NN, preferred_element_type=F32)
    odd = lax.dot_general(wave_scr[1], table_ref[1], NN, preferred_element_type=F32)
    near = even + odd
    far = even - odd
    at = pl.multiple_of(step * width, width)
    for half in range(2):
        for c in range(HALF_CYCLES):
            for field in range(FIELDS):
                row = half * LANES + (c * FIELDS + field) * MODES
                cycle = half * HALF_CYCLES + c
                out_ref[field, cycle, :, pl.ds(at, width)] = near[row : row + MODES]
                out_ref[field, cycle, :, pl.ds(HALF + at, width)] = far[row : row + MODES]


def whole(shape):
    return pl.BlockSpec(shape, lambda i: (0,) * len(shape))


def exchange(messages):
    return lax.all_to_all(messages, AXES, split_axis=0, concat_axis=0, tiled=True)


def on_device(fields, cycle_weights, legendre, inverses, pole_coeffs, pair_order):
    owner = lax.axis_index(AXES).astype(jnp.int32).reshape(1)
    smem = pl.BlockSpec(memory_space=pltpu.SMEM)
    grid_fields = jnp.transpose(fields, (1, 2, 0, 3))

    table, outgoing = pl.pallas_call(
        forward_kernel,
        grid=(SLOTS,),
        in_specs=[
            smem,
            whole((SLOTS, LANES)),
            whole((FIELDS, CYCLES, MODES, LONS)),
        ],
        out_specs=[
            pl.BlockSpec((2, 2 * DEVS, HALF), lambda i: (0, i, 0)),
            pl.BlockSpec((DEVS, SUB, LANES), lambda i: (0, i, 0)),
        ],
        out_shape=[
            jax.ShapeDtypeStruct((2, HALF, HALF), BF16),
            jax.ShapeDtypeStruct((DEVS, ROWS, LANES), BF16),
        ],
        scratch_shapes=[
            pltpu.VMEM((2, 256, HALF), BF16),
            pltpu.VMEM((DEVS * SUB, LANES), F32),
        ],
        name="forward",
    )(cycle_weights, pair_order.reshape(SLOTS, LANES), grid_fields)

    incoming = exchange(outgoing)

    leg = jnp.transpose(legendre, (1, 2, 0))
    inv = jnp.transpose(inverses, (2, 0, 3, 4, 5, 1, 6))
    inv = jnp.pad(inv, ((0, 0),) * 6 + ((0, WIDE - COLS),))

    returning = pl.pallas_call(
        middle_kernel,
        grid=(SLOTS,),
        in_specs=[
            smem,
            smem,
            smem,
            pl.BlockSpec((DEVS, SUB, LANES), lambda i: (0, i, 0)),
            pl.BlockSpec((1, COLS, NLAT), lambda i: (i, 0, 0)),
            pl.BlockSpec((1, 2, 2, 3, 3, MODES, WIDE), lambda i: (i, 0, 0, 0, 0, 0, 0)),
        ],
        out_specs=pl.BlockSpec((DEVS, SUB, LANES), lambda i: (0, i, 0)),
        out_shape=jax.ShapeDtypeStruct((DEVS, ROWS, LANES), BF16),
        scratch_shapes=[
            pltpu.VMEM((DEVS * SUB, LANES), F32),
            pltpu.VMEM((NLAT, LANES), F32),
        ],
        compiler_params=pltpu.CompilerParams(vmem_limit_bytes=50 << 20),
        name="middle",
    )(owner, pair_order, pole_coeffs, incoming, leg, inv)

    back = exchange(returning)

    width = 256
    result = pl.pallas_call(
        backward_kernel,
        grid=(HALF // width,),
        in_specs=[
            whole((DEVS, ROWS, LANES)),
            pl.BlockSpec((2, HALF, width), lambda i: (0, 0, i)),
        ],
        out_specs=whole((FIELDS, CYCLES, MODES, LONS)),
        out_shape=jax.ShapeDtypeStruct((FIELDS, CYCLES, MODES, LONS), F32),
        scratch_shapes=[
            pltpu.VMEM((DEVS * ROWS, LANES), F32),
            pltpu.VMEM((2, 256, HALF), BF16),
        ],
        compiler_params=pltpu.CompilerParams(vmem_limit_bytes=20 << 20),
        name="backward",
    )(back, table)
    return jnp.transpose(result, (2, 0, 1, 3))


def solution(mesh):
    return jax.shard_map(
        on_device,
        mesh=mesh,
        in_specs=(
            P(None, None, AXES, None),
            P(AXES),
            P(None, AXES, None),
            P(None, None, AXES, None, None, None, None),
            P(),
            P(),
        ),
        out_specs=P(None, None, AXES, None),
        check_vma=False,
    )
```

```python
import math

import jax
import jax.numpy as jnp
from jax import lax
from jax.experimental import pallas as pl
from jax.experimental.pallas import tpu as pltpu
from jax.sharding import PartitionSpec as P

ITERS = 3
ROTATION = 0.4
AXES = ("pole", "lat")
F32 = jnp.float32
BF16 = jnp.bfloat16
NT = (((1,), (1,)), ((), ()))
NN = (((1,), (0,)), ((), ()))

MODES, FIELDS, CYCLES, LONS = 8, 3, 10, 2560
DEVS, SLOTS, WAVES = 128, 5, 1280
HALF = LONS // 2
NLAT = DEVS * CYCLES
COLS = WAVES + 1
WIDE = 1408
HALF_CYCLES = CYCLES // 2
ROWS = 40
LANES = 128
SUB = 8
GROUP = 24


def sin_cos(product):
    turns = jnp.floor(product * (4.0 / LONS) + 0.5)
    angle = (product - turns * (LONS / 4.0)) * (2.0 * math.pi / LONS)
    z = angle * angle
    s = angle * (1.0 + z * (-1.0 / 6 + z * (1.0 / 120 + z * (-1.0 / 5040))))
    c = 1.0 + z * (-0.5 + z * (1.0 / 24 + z * (-1.0 / 720 + z * (1.0 / 40320))))
    quarter = turns.astype(jnp.int32) & 3
    swap = (quarter & 1) == 1
    sine = jnp.where(swap, c, s)
    cosine = jnp.where(swap, s, c)
    sine = jnp.where(quarter >= 2, -sine, sine)
    cosine = jnp.where((quarter == 1) | (quarter == 2), -cosine, cosine)
    return sine, cosine


def forward_kernel(weight_ref, pair_ref, field_ref, table_ref, send_ref, grid_scr, pack_scr):
    slot = pl.program_id(0)

    @pl.when(slot == 0)
    def _():
        for half in range(2):
            for c in range(HALF_CYCLES):
                cycle = half * HALF_CYCLES + c
                weight = weight_ref[cycle]
                for field in range(FIELDS):
                    row = half * LANES + (c * FIELDS + field) * MODES
                    near = field_ref[field, cycle, :, :HALF].astype(F32) * weight
                    far = field_ref[field, cycle, :, HALF:].astype(F32) * weight
                    grid_scr[0, row : row + MODES, :] = (near + far).astype(BF16)
                    grid_scr[1, row : row + MODES, :] = (near - far).astype(BF16)
            row = half * LANES + FIELDS * HALF_CYCLES * MODES
            grid_scr[:, row : (half + 1) * LANES, :] = jnp.zeros((2, MODES, HALF), BF16)

    place = lax.broadcasted_iota(jnp.int32, (SUB, LANES), 1) * SLOTS + slot
    pair = jnp.zeros((SUB, LANES), jnp.int32)
    for row in range(SLOTS):
        source = jnp.broadcast_to(pair_ref[row : row + 1, :], (SUB, LANES))
        found = jnp.take_along_axis(source, place & (LANES - 1), axis=1)
        pair = jnp.where(place >> 7 == row, found, pair)
    is_even = (pair & 1) == 0
    even = jnp.where(is_even, pair, WAVES - 1 - pair)
    waves = (even, WAVES - 1 - even)

    def down(row):
        return jnp.transpose(jnp.broadcast_to(row[:1], (LANES, LANES)))

    turns = [[down(v) for v in sin_cos(wave.astype(F32) * float(LANES))] for wave in waves]
    signs = [down(jnp.where((wave & 2) == 0, 1.0, -1.0).astype(F32)) for wave in waves]
    even = down(even.astype(F32))

    lane = lax.broadcasted_iota(jnp.int32, (1, LANES), 1)
    alternate = jnp.where((lane & 1) == 0, 1.0, -1.0)
    to_odd_sin, to_odd_cos = (v * alternate for v in sin_cos(lane.astype(F32)))
    scale = 1.0 / math.sqrt(LONS)
    for chunk in range(4):
        part = slice(chunk * 32, (chunk + 1) * 32)
        sine, cosine = sin_cos(even[part] * lane.astype(F32))
        cosine, minus = cosine * scale, sine * -scale
        starts = (
            (cosine, minus),
            (cosine * to_odd_cos + minus * to_odd_sin, cosine * to_odd_sin - minus * to_odd_cos),
        )
        for parity in range(2):
            cosine, minus = starts[parity]
            step_sin, step_cos = (v[part] for v in turns[parity])
            sign = signs[parity][part].astype(BF16)
            low = slice(LANES + chunk * 32, LANES + (chunk + 1) * 32)
            for block in range(HALF // LANES // 2):
                at = slice(block * LANES, (block + 1) * LANES)
                later = slice(HALF // 2 + block * LANES, HALF // 2 + (block + 1) * LANES)
                re, im = cosine.astype(BF16), minus.astype(BF16)
                table_ref[parity, part, at] = re
                table_ref[parity, low, at] = im
                table_ref[parity, part, later] = im * sign if parity else re * sign
                table_ref[parity, low, later] = -re * sign if parity else im * sign
                cosine, minus = (
                    cosine * step_cos + minus * step_sin,
                    minus * step_cos - cosine * step_sin,
                )
    for parity in range(2):
        coeffs = lax.dot_general(table_ref[parity], grid_scr[parity], NT, preferred_element_type=F32)
        for part in range(2):
            x = parity * 2 + part
            for half in range(2):
                piece = coeffs[part * LANES : (part + 1) * LANES, half * LANES : (half + 1) * LANES]
                if x:
                    piece = pltpu.roll(piece, GROUP * x, axis=1)
                pack_scr[pl.ds(x * 2 + half, DEVS, stride=SUB), :] = piece
    send_ref[...] = pack_scr[...].reshape(DEVS, SUB, LANES).astype(BF16)


def shift_prev(v):
    return pltpu.roll(v, 1, axis=1)


def shift_next(v):
    return pltpu.roll(v, WIDE - 1, axis=1)


def coupling_weights(pair):
    offset = lax.broadcasted_iota(jnp.int32, (MODES, WIDE), 1)
    in_first = offset < WAVES - pair
    order_int = jnp.where(in_first, pair, WAVES - 1 - pair)
    degree = jnp.where(in_first, pair + offset, offset - 1)
    order_m = order_int.astype(F32)
    lower_n = degree.astype(F32)
    upper_n = lower_n + 1.0
    down_ratio = jnp.maximum(lower_n * lower_n - order_m * order_m, 0.0) / jnp.maximum(
        4.0 * lower_n * lower_n - 1.0, 1.0
    )
    up_ratio = jnp.maximum(upper_n * upper_n - order_m * order_m, 0.0) / (
        4.0 * upper_n * upper_n - 1.0
    )
    real = offset < COLS
    eps_down = jnp.where((degree > order_int) & real, ROTATION * jnp.sqrt(down_ratio), 0.0)
    eps_up = jnp.where((degree + 1 < WAVES) & real, ROTATION * jnp.sqrt(up_ratio), 0.0)
    return in_first, eps_down, eps_up


def lane_group(position):
    lane = lax.broadcasted_iota(jnp.int32, (DEVS, LANES), 1)
    lane = lane - (GROUP * position) % LANES
    lane = jnp.where(lane < 0, lane + LANES, lane)
    return lane < GROUP


def unpack_columns(recv_ref, pack_scr, cycle_scr):
    pack_scr[...] = recv_ref[...].astype(F32).reshape(DEVS * SUB, LANES)
    for half in range(2):
        rows = [pack_scr[pl.ds(x * 2 + half, DEVS, stride=SUB), :] for x in range(4)]
        for c in range(HALF_CYCLES):
            merged = rows[3]
            for x in range(3):
                merged = jnp.where(lane_group(c + x), rows[x], merged)
            if c:
                merged = pltpu.roll(merged, LANES - GROUP * c, axis=1)
            cycle_scr[pl.ds(half * HALF_CYCLES + c, DEVS, stride=CYCLES), :] = merged
    return jnp.concatenate(
        [jnp.transpose(cycle_scr[t * LANES : (t + 1) * LANES, :])[:96] for t in range(NLAT // LANES)], axis=1
    )


def analyse(column, leg_ref):
    last = leg_ref[WAVES:COLS, :].astype(F32)
    spec_last = jnp.sum(column * last, axis=1, keepdims=True)
    spec = lax.dot_general(column.astype(BF16), leg_ref[:WAVES, :], NT, preferred_element_type=F32)
    first_lane = lax.broadcasted_iota(jnp.int32, (96, LANES), 1) == 0
    return spec, jnp.where(first_lane, spec_last, 0.0)


def solve(rhs, inv_ref, pole_ref, eps_down, eps_up):
    def couple(cur_real, cur_imag):
        return (
            eps_down * shift_prev(cur_real) + eps_up * shift_next(cur_real),
            eps_down * shift_prev(cur_imag) + eps_up * shift_next(cur_imag),
        )

    def apply(pole, row, terms):
        real, imag = None, None
        for c, (re, im) in terms:
            inv_re = inv_ref[pole, 0, row, c]
            inv_im = inv_ref[pole, 1, row, c]
            add_re = inv_re * re - inv_im * im
            add_im = inv_re * im + inv_im * re
            real = add_re if real is None else real + add_re
            imag = add_im if imag is None else imag + add_im
        return real, imag

    combined = [[None, None] for _ in range(FIELDS)]
    for pole in range(2):
        base = [apply(pole, f, list(enumerate(rhs))) for f in range(FIELDS)]
        div, vort = base[1], base[2]
        for step in range(ITERS):
            to_div, to_vort = couple(*vort), couple(*div)
            fields = range(FIELDS) if step == ITERS - 1 else (1, 2)
            solution = {}
            for f in fields:
                re, im = apply(pole, f, [(1, to_div), (2, to_vort)])
                solution[f] = (base[f][0] - re, base[f][1] - im)
            div, vort = solution[1], solution[2]
        beta_re = pole_ref[pole, 0]
        beta_im = pole_ref[pole, 1]
        for f in range(FIELDS):
            re, im = solution[f]
            add_re = beta_re * re - beta_im * im
            add_im = beta_re * im + beta_im * re
            combined[f][0] = add_re if pole == 0 else combined[f][0] + add_re
            combined[f][1] = add_im if pole == 0 else combined[f][1] + add_im
    return [combined[f][part] for part in range(2) for f in range(FIELDS)]


def synthesize(groups, in_even, pair, leg_ref):
    even = jnp.concatenate([jnp.where(in_even, g, 0.0) for g in groups], axis=0)
    odd = jnp.concatenate([jnp.where(in_even, 0.0, g) for g in groups], axis=0)
    both = jnp.concatenate([even, odd], axis=0).astype(BF16)
    synth = lax.dot_general(both[:, :WAVES], leg_ref[:WAVES, :], NN, preferred_element_type=F32)
    synth = synth + both[:, WAVES : WAVES + 1].astype(F32) * leg_ref[WAVES:COLS, :].astype(F32)
    row_at = lax.broadcasted_iota(jnp.int32, (96, NLAT), 0)
    return jnp.where((row_at < 48) & (pair == 0), synth, synth * 2.0)


def pack_messages(synth, send_ref, pack_scr, cycle_scr):
    synth = jnp.concatenate([synth, jnp.zeros((32, NLAT), F32)], axis=0)
    for t in range(NLAT // LANES):
        cycle_scr[t * LANES : (t + 1) * LANES, :] = jnp.transpose(synth[:, t * LANES : (t + 1) * LANES])
    for half in range(2):
        turned = []
        for c in range(HALF_CYCLES):
            values = cycle_scr[pl.ds(half * HALF_CYCLES + c, DEVS, stride=CYCLES), :]
            turned.append(pltpu.roll(values, GROUP * c, axis=1) if c else values)
        for x in range(4):
            merged = turned[HALF_CYCLES - 1]
            for c in range(HALF_CYCLES - 1):
                merged = jnp.where(lane_group(c + x), turned[c], merged)
            pack_scr[pl.ds(x * 2 + half, DEVS, stride=SUB), :] = merged
    send_ref[...] = pack_scr[...].reshape(DEVS, SUB, LANES).astype(BF16)


def middle_kernel(
    owner_ref, pair_ref, pole_ref, recv_ref, leg_hbm, inv_hbm, send_ref,
    leg_scr, inv_scr, spec_scr, pack_in, cycle_in, pack_out, cycle_out, leg_sem, inv_sem,
):
    step = pl.program_id(0)

    def leg_copy(slot):
        return pltpu.make_async_copy(leg_hbm.at[slot], leg_scr.at[slot], leg_sem.at[slot])

    def inv_copy(slot):
        return pltpu.make_async_copy(inv_hbm.at[slot], inv_scr.at[slot], inv_sem.at[slot])

    def store_spec(spec, spec_last):
        spec_scr[:, :WAVES] = spec
        spec_scr[:, WAVES:] = spec_last

    def right_side(slot):
        pair = pair_ref[owner_ref[0] * SLOTS + slot]
        in_first, eps_down, eps_up = coupling_weights(pair)
        in_even = in_first == ((pair & 1) == 0)
        rhs = [
            jnp.where(in_even, spec_scr[g * MODES : (g + 1) * MODES, :], spec_scr[48 + g * MODES : 56 + g * MODES, :])
            for g in range(6)
        ]
        return pair, in_even, [(rhs[f], rhs[3 + f]) for f in range(FIELDS)], eps_down, eps_up

    @pl.when(step == 0)
    def _():
        leg_copy(0).start()
        inv_copy(0).start()
        leg_copy(1).start()
        column = unpack_columns(recv_ref, pack_in, cycle_in)
        leg_copy(0).wait()
        inv_copy(1).start()
        leg_copy(2).start()
        store_spec(*analyse(column, leg_scr.at[0]))

    @pl.when((step > 0) & (step < SLOTS))
    def _():
        inv_copy(step - 1).wait()
        leg_copy(step).wait()

        @pl.when(step + 1 < SLOTS)
        def _():
            inv_copy(step + 1).start()

        @pl.when(step + 2 < SLOTS)
        def _():
            leg_copy(step + 2).start()

        pair, in_even, rhs, eps_down, eps_up = right_side(step - 1)
        column = unpack_columns(recv_ref, pack_in, cycle_in)
        spec = analyse(column, leg_scr.at[step])
        groups = solve(rhs, inv_scr.at[step - 1], pole_ref, eps_down, eps_up)
        store_spec(*spec)
        synth = synthesize(groups, in_even, pair, leg_scr.at[step - 1])
        pack_messages(synth, send_ref, pack_out, cycle_out)

    @pl.when(step == SLOTS)
    def _():
        inv_copy(SLOTS - 1).wait()
        pair, in_even, rhs, eps_down, eps_up = right_side(SLOTS - 1)
        groups = solve(rhs, inv_scr.at[SLOTS - 1], pole_ref, eps_down, eps_up)
        synth = synthesize(groups, in_even, pair, leg_scr.at[SLOTS - 1])
        pack_messages(synth, send_ref, pack_out, cycle_out)


def backward_kernel(recv_ref, table_ref, out_ref, pack_scr, wave_scr):
    step = pl.program_id(0)
    width = table_ref.shape[-1]

    @pl.when(step == 0)
    def _():
        pack_scr[...] = recv_ref[...].astype(F32).reshape(DEVS * ROWS, LANES)
        for slot in range(SLOTS):
            for x in range(4):
                parity, part = x // 2, x % 2
                at = (slot * 2 + part) * LANES
                for half in range(2):
                    row = slot * SUB + x * 2 + half
                    turned = jnp.transpose(pack_scr[pl.ds(row, DEVS, stride=ROWS), :])
                    if x:
                        turned = jnp.concatenate([turned[GROUP * x :], turned[: GROUP * x]], axis=0)
                    wave_scr[parity, half * LANES : (half + 1) * LANES, at : at + LANES] = turned.astype(BF16)

    even = lax.dot_general(wave_scr[0], table_ref[0], NN, preferred_element_type=F32)
    odd = lax.dot_general(wave_scr[1], table_ref[1], NN, preferred_element_type=F32)
    near = even + odd
    far = even - odd
    at = pl.multiple_of(step * width, width)
    for half in range(2):
        for c in range(HALF_CYCLES):
            for field in range(FIELDS):
                row = half * LANES + (c * FIELDS + field) * MODES
                cycle = half * HALF_CYCLES + c
                out_ref[field, cycle, :, pl.ds(at, width)] = near[row : row + MODES]
                out_ref[field, cycle, :, pl.ds(HALF + at, width)] = far[row : row + MODES]


def whole(shape):
    return pl.BlockSpec(shape, lambda i: (0,) * len(shape))


def exchange(messages):
    return lax.all_to_all(messages, AXES, split_axis=0, concat_axis=0, tiled=True)


def on_device(fields, cycle_weights, legendre, inverses, pole_coeffs, pair_order):
    owner = lax.axis_index(AXES).astype(jnp.int32).reshape(1)
    smem = pl.BlockSpec(memory_space=pltpu.SMEM)
    grid_fields = jnp.transpose(fields, (1, 2, 0, 3))

    table, outgoing = pl.pallas_call(
        forward_kernel,
        grid=(SLOTS,),
        in_specs=[
            smem,
            whole((SLOTS, LANES)),
            whole((FIELDS, CYCLES, MODES, LONS)),
        ],
        out_specs=[
            pl.BlockSpec((2, 2 * DEVS, HALF), lambda i: (0, i, 0)),
            pl.BlockSpec((DEVS, SUB, LANES), lambda i: (0, i, 0)),
        ],
        out_shape=[
            jax.ShapeDtypeStruct((2, HALF, HALF), BF16),
            jax.ShapeDtypeStruct((DEVS, ROWS, LANES), BF16),
        ],
        scratch_shapes=[
            pltpu.VMEM((2, 256, HALF), BF16),
            pltpu.VMEM((DEVS * SUB, LANES), F32),
        ],
        name="forward",
    )(cycle_weights, pair_order.reshape(SLOTS, LANES), grid_fields)

    incoming = exchange(outgoing)

    leg = jnp.transpose(legendre, (1, 2, 0))
    inv = jnp.transpose(inverses, (2, 0, 3, 4, 5, 1, 6))
    inv = jnp.pad(inv, ((0, 0),) * 6 + ((0, WIDE - COLS),))

    anywhere = pl.BlockSpec(memory_space=pl.ANY)
    returning = pl.pallas_call(
        middle_kernel,
        grid=(SLOTS + 1,),
        in_specs=[
            smem,
            smem,
            smem,
            pl.BlockSpec((DEVS, SUB, LANES), lambda i: (0, jnp.minimum(i, SLOTS - 1), 0)),
            anywhere,
            anywhere,
        ],
        out_specs=pl.BlockSpec((DEVS, SUB, LANES), lambda i: (0, jnp.maximum(i - 1, 0), 0)),
        out_shape=jax.ShapeDtypeStruct((DEVS, ROWS, LANES), BF16),
        scratch_shapes=[
            pltpu.VMEM((SLOTS, COLS, NLAT), BF16),
            pltpu.VMEM((SLOTS, 2, 2, 3, 3, MODES, WIDE), F32),
            pltpu.VMEM((96, WIDE), F32),
            pltpu.VMEM((DEVS * SUB, LANES), F32),
            pltpu.VMEM((NLAT, LANES), F32),
            pltpu.VMEM((DEVS * SUB, LANES), F32),
            pltpu.VMEM((NLAT, LANES), F32),
            pltpu.SemaphoreType.DMA((SLOTS,)),
            pltpu.SemaphoreType.DMA((SLOTS,)),
        ],
        compiler_params=pltpu.CompilerParams(vmem_limit_bytes=50 << 20),
        name="middle",
    )(owner, pair_order, pole_coeffs, incoming, leg, inv)

    back = exchange(returning)

    width = 256
    result = pl.pallas_call(
        backward_kernel,
        grid=(HALF // width,),
        in_specs=[
            whole((DEVS, ROWS, LANES)),
            pl.BlockSpec((2, HALF, width), lambda i: (0, 0, i)),
        ],
        out_specs=whole((FIELDS, CYCLES, MODES, LONS)),
        out_shape=jax.ShapeDtypeStruct((FIELDS, CYCLES, MODES, LONS), F32),
        scratch_shapes=[
            pltpu.VMEM((DEVS * ROWS, LANES), F32),
            pltpu.VMEM((2, 256, HALF), BF16),
        ],
        compiler_params=pltpu.CompilerParams(vmem_limit_bytes=20 << 20),
        name="backward",
    )(back, table)
    return jnp.transpose(result, (2, 0, 1, 3))


def solution(mesh):
    return jax.shard_map(
        on_device,
        mesh=mesh,
        in_specs=(
            P(None, None, AXES, None),
            P(AXES),
            P(None, AXES, None),
            P(None, None, AXES, None, None, None, None),
            P(),
            P(),
        ),
        out_specs=P(None, None, AXES, None),
        check_vma=False,
    )
```

```python
import math

import jax
import jax.numpy as jnp
from jax import lax
from jax.experimental import pallas as pl
from jax.experimental.pallas import tpu as pltpu
from jax.sharding import PartitionSpec as P

ITERS = 3
ROTATION = 0.4
AXES = ("pole", "lat")
F32 = jnp.float32
BF16 = jnp.bfloat16
NT = (((1,), (1,)), ((), ()))
NN = (((1,), (0,)), ((), ()))

MODES, FIELDS, CYCLES, LONS = 8, 3, 10, 2560
DEVS, SLOTS, WAVES = 128, 5, 1280
HALF = LONS // 2
NLAT = DEVS * CYCLES
COLS = WAVES + 1
WIDE = 1408
HALF_CYCLES = CYCLES // 2
ROWS = 40
LANES = 128
SUB = 8
GROUP = 24


def sin_cos(product):
    turns = jnp.floor(product * (4.0 / LONS) + 0.5)
    angle = (product - turns * (LONS / 4.0)) * (2.0 * math.pi / LONS)
    z = angle * angle
    s = angle * (1.0 + z * (-1.0 / 6 + z * (1.0 / 120 + z * (-1.0 / 5040))))
    c = 1.0 + z * (-0.5 + z * (1.0 / 24 + z * (-1.0 / 720 + z * (1.0 / 40320))))
    quarter = turns.astype(jnp.int32) & 3
    swap = (quarter & 1) == 1
    sine = jnp.where(swap, c, s)
    cosine = jnp.where(swap, s, c)
    sine = jnp.where(quarter >= 2, -sine, sine)
    cosine = jnp.where((quarter == 1) | (quarter == 2), -cosine, cosine)
    return sine, cosine


def forward_kernel(weight_ref, pair_ref, field_ref, table_ref, send_ref, grid_scr, pack_scr):
    slot = pl.program_id(0)

    @pl.when(slot == 0)
    def _():
        for half in range(2):
            for c in range(HALF_CYCLES):
                cycle = half * HALF_CYCLES + c
                weight = weight_ref[cycle]
                for field in range(FIELDS):
                    row = half * LANES + (c * FIELDS + field) * MODES
                    near = field_ref[field, cycle, :, :HALF].astype(F32) * weight
                    far = field_ref[field, cycle, :, HALF:].astype(F32) * weight
                    grid_scr[0, row : row + MODES, :] = (near + far).astype(BF16)
                    grid_scr[1, row : row + MODES, :] = (near - far).astype(BF16)
            row = half * LANES + FIELDS * HALF_CYCLES * MODES
            grid_scr[:, row : (half + 1) * LANES, :] = jnp.zeros((2, MODES, HALF), BF16)

    place = lax.broadcasted_iota(jnp.int32, (SUB, LANES), 1) * SLOTS + slot
    pair = jnp.zeros((SUB, LANES), jnp.int32)
    for row in range(SLOTS):
        source = jnp.broadcast_to(pair_ref[row : row + 1, :], (SUB, LANES))
        found = jnp.take_along_axis(source, place & (LANES - 1), axis=1)
        pair = jnp.where(place >> 7 == row, found, pair)
    is_even = (pair & 1) == 0
    even = jnp.where(is_even, pair, WAVES - 1 - pair)
    waves = (even, WAVES - 1 - even)

    def down(row):
        return jnp.transpose(jnp.broadcast_to(row[:1], (LANES, LANES)))

    turns = [[down(v) for v in sin_cos(wave.astype(F32) * float(LANES))] for wave in waves]
    signs = [down(jnp.where((wave & 2) == 0, 1.0, -1.0).astype(F32)) for wave in waves]
    even = down(even.astype(F32))

    lane = lax.broadcasted_iota(jnp.int32, (1, LANES), 1)
    alternate = jnp.where((lane & 1) == 0, 1.0, -1.0)
    to_odd_sin, to_odd_cos = (v * alternate for v in sin_cos(lane.astype(F32)))
    scale = 1.0 / math.sqrt(LONS)
    for chunk in range(4):
        part = slice(chunk * 32, (chunk + 1) * 32)
        sine, cosine = sin_cos(even[part] * lane.astype(F32))
        cosine, minus = cosine * scale, sine * -scale
        starts = (
            (cosine, minus),
            (cosine * to_odd_cos + minus * to_odd_sin, cosine * to_odd_sin - minus * to_odd_cos),
        )
        for parity in range(2):
            cosine, minus = starts[parity]
            step_sin, step_cos = (v[part] for v in turns[parity])
            sign = signs[parity][part].astype(BF16)
            low = slice(LANES + chunk * 32, LANES + (chunk + 1) * 32)
            for block in range(HALF // LANES // 2):
                at = slice(block * LANES, (block + 1) * LANES)
                later = slice(HALF // 2 + block * LANES, HALF // 2 + (block + 1) * LANES)
                re, im = cosine.astype(BF16), minus.astype(BF16)
                table_ref[parity, part, at] = re
                table_ref[parity, low, at] = im
                table_ref[parity, part, later] = im * sign if parity else re * sign
                table_ref[parity, low, later] = -re * sign if parity else im * sign
                cosine, minus = (
                    cosine * step_cos + minus * step_sin,
                    minus * step_cos - cosine * step_sin,
                )
    for parity in range(2):
        coeffs = lax.dot_general(table_ref[parity], grid_scr[parity], NT, preferred_element_type=F32)
        for part in range(2):
            x = parity * 2 + part
            for half in range(2):
                piece = coeffs[part * LANES : (part + 1) * LANES, half * LANES : (half + 1) * LANES]
                if x:
                    piece = pltpu.roll(piece, GROUP * x, axis=1)
                pack_scr[pl.ds(x * 2 + half, DEVS, stride=SUB), :] = piece
    send_ref[...] = pack_scr[...].reshape(DEVS, SUB, LANES).astype(BF16)


def shift_prev(v):
    return pltpu.roll(v, 1, axis=1)


def shift_next(v):
    return pltpu.roll(v, WIDE - 1, axis=1)


def coupling_weights(pair):
    offset = lax.broadcasted_iota(jnp.int32, (MODES, WIDE), 1)
    in_first = offset < WAVES - pair
    order_int = jnp.where(in_first, pair, WAVES - 1 - pair)
    degree = jnp.where(in_first, pair + offset, offset - 1)
    order_m = order_int.astype(F32)
    lower_n = degree.astype(F32)
    upper_n = lower_n + 1.0
    down_ratio = jnp.maximum(lower_n * lower_n - order_m * order_m, 0.0) / jnp.maximum(
        4.0 * lower_n * lower_n - 1.0, 1.0
    )
    up_ratio = jnp.maximum(upper_n * upper_n - order_m * order_m, 0.0) / (
        4.0 * upper_n * upper_n - 1.0
    )
    real = offset < COLS
    eps_down = jnp.where((degree > order_int) & real, ROTATION * jnp.sqrt(down_ratio), 0.0)
    eps_up = jnp.where((degree + 1 < WAVES) & real, ROTATION * jnp.sqrt(up_ratio), 0.0)
    return in_first, eps_down, eps_up


def lane_group(position):
    lane = lax.broadcasted_iota(jnp.int32, (DEVS, LANES), 1)
    lane = lane - (GROUP * position) % LANES
    lane = jnp.where(lane < 0, lane + LANES, lane)
    return lane < GROUP


def unpack_columns(recv_ref, pack_scr, cycle_scr):
    pack_scr[...] = recv_ref[...].astype(F32).reshape(DEVS * SUB, LANES)
    for half in range(2):
        rows = [pack_scr[pl.ds(x * 2 + half, DEVS, stride=SUB), :] for x in range(4)]
        for c in range(HALF_CYCLES):
            merged = rows[3]
            for x in range(3):
                merged = jnp.where(lane_group(c + x), rows[x], merged)
            if c:
                merged = pltpu.roll(merged, LANES - GROUP * c, axis=1)
            cycle_scr[pl.ds(half * HALF_CYCLES + c, DEVS, stride=CYCLES), :] = merged
    return jnp.concatenate(
        [jnp.transpose(cycle_scr[t * LANES : (t + 1) * LANES, :])[:96] for t in range(NLAT // LANES)], axis=1
    )


def analyse(column, leg_ref):
    last = leg_ref[WAVES:COLS, :].astype(F32)
    spec_last = jnp.sum(column * last, axis=1, keepdims=True)
    spec = lax.dot_general(column.astype(BF16), leg_ref[:WAVES, :], NT, preferred_element_type=F32)
    first_lane = lax.broadcasted_iota(jnp.int32, (96, LANES), 1) == 0
    return spec, jnp.where(first_lane, spec_last, 0.0)


def solve(rhs, inv_ref, pole_ref, eps_down, eps_up):
    def couple(cur_real, cur_imag):
        return (
            eps_down * shift_prev(cur_real) + eps_up * shift_next(cur_real),
            eps_down * shift_prev(cur_imag) + eps_up * shift_next(cur_imag),
        )

    def apply(pole, row, terms):
        real, imag = None, None
        for c, (re, im) in terms:
            inv_re = inv_ref[pole, 0, row, c]
            inv_im = inv_ref[pole, 1, row, c]
            add_re = inv_re * re - inv_im * im
            add_im = inv_re * im + inv_im * re
            real = add_re if real is None else real + add_re
            imag = add_im if imag is None else imag + add_im
        return real, imag

    combined = [[None, None] for _ in range(FIELDS)]
    for pole in range(2):
        base = [apply(pole, f, list(enumerate(rhs))) for f in range(FIELDS)]
        div, vort = base[1], base[2]
        for step in range(ITERS):
            to_div, to_vort = couple(*vort), couple(*div)
            fields = range(FIELDS) if step == ITERS - 1 else (1, 2)
            solution = {}
            for f in fields:
                re, im = apply(pole, f, [(1, to_div), (2, to_vort)])
                solution[f] = (base[f][0] - re, base[f][1] - im)
            div, vort = solution[1], solution[2]
        beta_re = pole_ref[pole, 0]
        beta_im = pole_ref[pole, 1]
        for f in range(FIELDS):
            re, im = solution[f]
            add_re = beta_re * re - beta_im * im
            add_im = beta_re * im + beta_im * re
            combined[f][0] = add_re if pole == 0 else combined[f][0] + add_re
            combined[f][1] = add_im if pole == 0 else combined[f][1] + add_im
    return [combined[f][part] for part in range(2) for f in range(FIELDS)]


def synthesize(groups, in_even, pair, leg_ref):
    even = jnp.concatenate([jnp.where(in_even, g, 0.0) for g in groups], axis=0)
    odd = jnp.concatenate([jnp.where(in_even, 0.0, g) for g in groups], axis=0)
    both = jnp.concatenate([even, odd], axis=0).astype(BF16)
    synth = lax.dot_general(both[:, :WAVES], leg_ref[:WAVES, :], NN, preferred_element_type=F32)
    synth = synth + both[:, WAVES : WAVES + 1].astype(F32) * leg_ref[WAVES:COLS, :].astype(F32)
    row_at = lax.broadcasted_iota(jnp.int32, (96, NLAT), 0)
    return jnp.where((row_at < 48) & (pair == 0), synth, synth * 2.0)


def pack_messages(synth, send_ref, pack_scr, cycle_scr):
    synth = jnp.concatenate([synth, jnp.zeros((32, NLAT), F32)], axis=0)
    for t in range(NLAT // LANES):
        cycle_scr[t * LANES : (t + 1) * LANES, :] = jnp.transpose(synth[:, t * LANES : (t + 1) * LANES])
    for half in range(2):
        turned = []
        for c in range(HALF_CYCLES):
            values = cycle_scr[pl.ds(half * HALF_CYCLES + c, DEVS, stride=CYCLES), :]
            turned.append(pltpu.roll(values, GROUP * c, axis=1) if c else values)
        for x in range(4):
            merged = turned[HALF_CYCLES - 1]
            for c in range(HALF_CYCLES - 1):
                merged = jnp.where(lane_group(c + x), turned[c], merged)
            pack_scr[pl.ds(x * 2 + half, DEVS, stride=SUB), :] = merged
    send_ref[...] = pack_scr[...].reshape(DEVS, SUB, LANES).astype(BF16)


def middle_kernel(
    owner_ref, pair_ref, pole_ref, recv_ref, leg_first, leg_hbm, inv_hbm, send_ref,
    leg_scr, inv_scr, spec_scr, pack_in, cycle_in, pack_out, cycle_out, leg_sem, inv_sem,
):
    step = pl.program_id(0)

    def leg_copy(slot):
        return pltpu.make_async_copy(leg_hbm.at[slot], leg_scr.at[slot], leg_sem.at[slot])

    def first_copy():
        return pltpu.make_async_copy(leg_first, leg_scr.at[0], leg_sem.at[0])

    def inv_copy(slot):
        return pltpu.make_async_copy(inv_hbm.at[slot], inv_scr.at[slot], inv_sem.at[slot])

    def store_spec(spec, spec_last):
        spec_scr[:, :WAVES] = spec
        spec_scr[:, WAVES:] = spec_last

    def right_side(slot):
        pair = pair_ref[owner_ref[0] * SLOTS + slot]
        in_first, eps_down, eps_up = coupling_weights(pair)
        in_even = in_first == ((pair & 1) == 0)
        rhs = [
            jnp.where(in_even, spec_scr[g * MODES : (g + 1) * MODES, :], spec_scr[48 + g * MODES : 56 + g * MODES, :])
            for g in range(6)
        ]
        return pair, in_even, [(rhs[f], rhs[3 + f]) for f in range(FIELDS)], eps_down, eps_up

    @pl.when(step == 0)
    def _():
        first_copy().start()
        inv_copy(0).start()
        leg_copy(1).start()
        column = unpack_columns(recv_ref, pack_in, cycle_in)
        first_copy().wait()
        inv_copy(1).start()
        leg_copy(2).start()
        store_spec(*analyse(column, leg_scr.at[0]))

    @pl.when((step > 0) & (step < SLOTS))
    def _():
        inv_copy(step - 1).wait()
        leg_copy(step).wait()

        @pl.when(step + 1 < SLOTS)
        def _():
            inv_copy(step + 1).start()

        @pl.when(step + 2 < SLOTS)
        def _():
            leg_copy(step + 2).start()

        pair, in_even, rhs, eps_down, eps_up = right_side(step - 1)
        column = unpack_columns(recv_ref, pack_in, cycle_in)
        spec = analyse(column, leg_scr.at[step])
        groups = solve(rhs, inv_scr.at[step - 1], pole_ref, eps_down, eps_up)
        store_spec(*spec)
        synth = synthesize(groups, in_even, pair, leg_scr.at[step - 1])
        pack_messages(synth, send_ref, pack_out, cycle_out)

    @pl.when(step == SLOTS)
    def _():
        inv_copy(SLOTS - 1).wait()
        pair, in_even, rhs, eps_down, eps_up = right_side(SLOTS - 1)
        groups = solve(rhs, inv_scr.at[SLOTS - 1], pole_ref, eps_down, eps_up)
        synth = synthesize(groups, in_even, pair, leg_scr.at[SLOTS - 1])
        pack_messages(synth, send_ref, pack_out, cycle_out)


def backward_kernel(recv_ref, table_ref, out_hbm, pack_scr, wave_scr, out_scr, out_sem):
    step = pl.program_id(0)
    width = table_ref.shape[-1]

    @pl.when(step == 0)
    def _():
        pack_scr[...] = recv_ref[...].astype(F32).reshape(DEVS * ROWS, LANES)
        for slot in range(SLOTS):
            for x in range(4):
                parity, part = x // 2, x % 2
                at = (slot * 2 + part) * LANES
                for half in range(2):
                    row = slot * SUB + x * 2 + half
                    turned = jnp.transpose(pack_scr[pl.ds(row, DEVS, stride=ROWS), :])
                    if x:
                        turned = jnp.concatenate([turned[GROUP * x :], turned[: GROUP * x]], axis=0)
                    wave_scr[parity, half * LANES : (half + 1) * LANES, at : at + LANES] = turned.astype(BF16)

    even = lax.dot_general(wave_scr[0], table_ref[0], NN, preferred_element_type=F32)
    odd = lax.dot_general(wave_scr[1], table_ref[1], NN, preferred_element_type=F32)
    near = even + odd
    far = even - odd
    slot = step % 2

    def leave(when):
        at = pl.multiple_of(when * width, width)
        return [
            pltpu.make_async_copy(
                out_scr.at[when % 2, side],
                out_hbm.at[:, :, :, pl.ds(side * HALF + at, width)],
                out_sem.at[when % 2, side],
            )
            for side in range(2)
        ]

    @pl.when(step >= 2)
    def _():
        for copy in leave(step - 2):
            copy.wait()

    for half in range(2):
        for c in range(HALF_CYCLES):
            for field in range(FIELDS):
                row = half * LANES + (c * FIELDS + field) * MODES
                cycle = half * HALF_CYCLES + c
                out_scr[slot, 0, field, cycle, :, :] = near[row : row + MODES]
                out_scr[slot, 1, field, cycle, :, :] = far[row : row + MODES]

    for copy in leave(step):
        copy.start()

    @pl.when(step == pl.num_programs(0) - 1)
    def _():
        for when in (step - 1, step):
            for copy in leave(when):
                copy.wait()


def whole(shape):
    return pl.BlockSpec(shape, lambda i: (0,) * len(shape))


def exchange(messages):
    return lax.all_to_all(messages, AXES, split_axis=0, concat_axis=0, tiled=True)


def on_device(fields, cycle_weights, legendre, inverses, pole_coeffs, pair_order):
    owner = lax.axis_index(AXES).astype(jnp.int32).reshape(1)
    smem = pl.BlockSpec(memory_space=pltpu.SMEM)
    grid_fields = jnp.transpose(fields, (1, 2, 0, 3))

    table, outgoing = pl.pallas_call(
        forward_kernel,
        grid=(SLOTS,),
        in_specs=[
            smem,
            whole((SLOTS, LANES)),
            whole((FIELDS, CYCLES, MODES, LONS)),
        ],
        out_specs=[
            pl.BlockSpec((2, 2 * DEVS, HALF), lambda i: (0, i, 0)),
            pl.BlockSpec((DEVS, SUB, LANES), lambda i: (0, i, 0)),
        ],
        out_shape=[
            jax.ShapeDtypeStruct((2, HALF, HALF), BF16),
            jax.ShapeDtypeStruct((DEVS, ROWS, LANES), BF16),
        ],
        scratch_shapes=[
            pltpu.VMEM((2, 256, HALF), BF16),
            pltpu.VMEM((DEVS * SUB, LANES), F32),
        ],
        name="forward",
    )(cycle_weights, pair_order.reshape(SLOTS, LANES), grid_fields)

    incoming = exchange(outgoing)

    leg = jnp.transpose(legendre, (1, 2, 0))
    inv = jnp.transpose(inverses, (2, 0, 3, 4, 5, 1, 6))
    inv = jnp.pad(inv, ((0, 0),) * 6 + ((0, WIDE - COLS),))

    anywhere = pl.BlockSpec(memory_space=pl.ANY)
    returning = pl.pallas_call(
        middle_kernel,
        grid=(SLOTS + 1,),
        in_specs=[
            smem,
            smem,
            smem,
            pl.BlockSpec((DEVS, SUB, LANES), lambda i: (0, jnp.minimum(i, SLOTS - 1), 0)),
            anywhere,
            anywhere,
            anywhere,
        ],
        out_specs=pl.BlockSpec((DEVS, SUB, LANES), lambda i: (0, jnp.maximum(i - 1, 0), 0)),
        out_shape=jax.ShapeDtypeStruct((DEVS, ROWS, LANES), BF16),
        scratch_shapes=[
            pltpu.VMEM((SLOTS, COLS, NLAT), BF16),
            pltpu.VMEM((SLOTS, 2, 2, 3, 3, MODES, WIDE), F32),
            pltpu.VMEM((96, WIDE), F32),
            pltpu.VMEM((DEVS * SUB, LANES), F32),
            pltpu.VMEM((NLAT, LANES), F32),
            pltpu.VMEM((DEVS * SUB, LANES), F32),
            pltpu.VMEM((NLAT, LANES), F32),
            pltpu.SemaphoreType.DMA((SLOTS,)),
            pltpu.SemaphoreType.DMA((SLOTS,)),
        ],
        compiler_params=pltpu.CompilerParams(vmem_limit_bytes=46 << 20),
        name="middle",
    )(owner, pair_order, pole_coeffs, incoming, leg[0], leg, inv)

    back = exchange(returning)

    width = 256
    result = pl.pallas_call(
        backward_kernel,
        grid=(HALF // width,),
        in_specs=[
            whole((DEVS, ROWS, LANES)),
            pl.BlockSpec((2, HALF, width), lambda i: (0, 0, i)),
        ],
        out_specs=anywhere,
        out_shape=jax.ShapeDtypeStruct((FIELDS, CYCLES, MODES, LONS), F32),
        scratch_shapes=[
            pltpu.VMEM((DEVS * ROWS, LANES), F32),
            pltpu.VMEM((2, 256, HALF), BF16),
            pltpu.VMEM((2, 2, FIELDS, CYCLES, MODES, width), F32),
            pltpu.SemaphoreType.DMA((2, 2)),
        ],
        compiler_params=pltpu.CompilerParams(vmem_limit_bytes=20 << 20),
        name="backward",
    )(back, table)
    return jnp.transpose(result, (2, 0, 1, 3))


def solution(mesh):
    return jax.shard_map(
        on_device,
        mesh=mesh,
        in_specs=(
            P(None, None, AXES, None),
            P(AXES),
            P(None, AXES, None),
            P(None, None, AXES, None, None, None, None),
            P(),
            P(),
        ),
        out_specs=P(None, None, AXES, None),
        check_vma=False,
    )
```

```python
import math

import jax
import jax.numpy as jnp
from jax import lax
from jax.experimental import pallas as pl
from jax.experimental.pallas import tpu as pltpu
from jax.sharding import PartitionSpec as P

ITERS = 3
ROTATION = 0.4
AXES = ("pole", "lat")
F32 = jnp.float32
BF16 = jnp.bfloat16
NT = (((1,), (1,)), ((), ()))
NN = (((1,), (0,)), ((), ()))

MODES, FIELDS, CYCLES, LONS = 8, 3, 10, 2560
DEVS, SLOTS, WAVES = 128, 5, 1280
HALF = LONS // 2
NLAT = DEVS * CYCLES
COLS = WAVES + 1
WIDE = 1408
HALF_CYCLES = CYCLES // 2
ROWS = 40
LANES = 128
SUB = 8
GROUP = 24


def sin_cos(product):
    turns = jnp.floor(product * (4.0 / LONS) + 0.5)
    angle = (product - turns * (LONS / 4.0)) * (2.0 * math.pi / LONS)
    z = angle * angle
    s = angle * (1.0 + z * (-1.0 / 6 + z * (1.0 / 120 + z * (-1.0 / 5040))))
    c = 1.0 + z * (-0.5 + z * (1.0 / 24 + z * (-1.0 / 720 + z * (1.0 / 40320))))
    quarter = turns.astype(jnp.int32) & 3
    swap = (quarter & 1) == 1
    sine = jnp.where(swap, c, s)
    cosine = jnp.where(swap, s, c)
    sine = jnp.where(quarter >= 2, -sine, sine)
    cosine = jnp.where((quarter == 1) | (quarter == 2), -cosine, cosine)
    return sine, cosine


def forward_kernel(weight_ref, pair_ref, field_ref, table_ref, send_ref, grid_scr, pack_scr):
    slot = pl.program_id(0)

    @pl.when(slot == 0)
    def _():
        for half in range(2):
            for c in range(HALF_CYCLES):
                cycle = half * HALF_CYCLES + c
                weight = weight_ref[cycle]
                for field in range(FIELDS):
                    row = half * LANES + (c * FIELDS + field) * MODES
                    near = field_ref[field, cycle, :, :HALF].astype(F32) * weight
                    far = field_ref[field, cycle, :, HALF:].astype(F32) * weight
                    grid_scr[0, row : row + MODES, :] = (near + far).astype(BF16)
                    grid_scr[1, row : row + MODES, :] = (near - far).astype(BF16)
            row = half * LANES + FIELDS * HALF_CYCLES * MODES
            grid_scr[:, row : (half + 1) * LANES, :] = jnp.zeros((2, MODES, HALF), BF16)

    place = lax.broadcasted_iota(jnp.int32, (SUB, LANES), 1) * SLOTS + slot
    pair = jnp.zeros((SUB, LANES), jnp.int32)
    for row in range(SLOTS):
        source = jnp.broadcast_to(pair_ref[row : row + 1, :], (SUB, LANES))
        found = jnp.take_along_axis(source, place & (LANES - 1), axis=1)
        pair = jnp.where(place >> 7 == row, found, pair)
    is_even = (pair & 1) == 0
    even = jnp.where(is_even, pair, WAVES - 1 - pair)
    waves = (even, WAVES - 1 - even)

    def down(row):
        return jnp.transpose(jnp.broadcast_to(row[:1], (LANES, LANES)))

    turns = [[down(v) for v in sin_cos(wave.astype(F32) * float(LANES))] for wave in waves]
    signs = [down(jnp.where((wave & 2) == 0, 1.0, -1.0).astype(F32)) for wave in waves]
    even = down(even.astype(F32))

    lane = lax.broadcasted_iota(jnp.int32, (1, LANES), 1)
    alternate = jnp.where((lane & 1) == 0, 1.0, -1.0)
    to_odd_sin, to_odd_cos = (v * alternate for v in sin_cos(lane.astype(F32)))
    scale = 1.0 / math.sqrt(LONS)
    for chunk in range(4):
        part = slice(chunk * 32, (chunk + 1) * 32)
        sine, cosine = sin_cos(even[part] * lane.astype(F32))
        cosine, minus = cosine * scale, sine * -scale
        starts = (
            (cosine, minus),
            (cosine * to_odd_cos + minus * to_odd_sin, cosine * to_odd_sin - minus * to_odd_cos),
        )
        for parity in range(2):
            cosine, minus = starts[parity]
            step_sin, step_cos = (v[part] for v in turns[parity])
            sign = signs[parity][part].astype(BF16)
            low = slice(LANES + chunk * 32, LANES + (chunk + 1) * 32)
            for block in range(HALF // LANES // 2):
                at = slice(block * LANES, (block + 1) * LANES)
                later = slice(HALF // 2 + block * LANES, HALF // 2 + (block + 1) * LANES)
                re, im = cosine.astype(BF16), minus.astype(BF16)
                table_ref[parity, part, at] = re
                table_ref[parity, low, at] = im
                table_ref[parity, part, later] = im * sign if parity else re * sign
                table_ref[parity, low, later] = -re * sign if parity else im * sign
                cosine, minus = (
                    cosine * step_cos + minus * step_sin,
                    minus * step_cos - cosine * step_sin,
                )
    for parity in range(2):
        coeffs = lax.dot_general(table_ref[parity], grid_scr[parity], NT, preferred_element_type=F32)
        for part in range(2):
            x = parity * 2 + part
            for half in range(2):
                piece = coeffs[part * LANES : (part + 1) * LANES, half * LANES : (half + 1) * LANES]
                if x:
                    piece = pltpu.roll(piece, GROUP * x, axis=1)
                pack_scr[pl.ds(x * 2 + half, DEVS, stride=SUB), :] = piece
    send_ref[...] = pack_scr[...].reshape(DEVS, SUB, LANES).astype(BF16)


def shift_prev(v):
    return pltpu.roll(v, 1, axis=1)


def shift_next(v):
    return pltpu.roll(v, WIDE - 1, axis=1)


def coupling_weights(pair):
    offset = lax.broadcasted_iota(jnp.int32, (MODES, WIDE), 1)
    in_first = offset < WAVES - pair
    order_int = jnp.where(in_first, pair, WAVES - 1 - pair)
    degree = jnp.where(in_first, pair + offset, offset - 1)
    order_m = order_int.astype(F32)
    lower_n = degree.astype(F32)
    upper_n = lower_n + 1.0
    down_ratio = jnp.maximum(lower_n * lower_n - order_m * order_m, 0.0) / jnp.maximum(
        4.0 * lower_n * lower_n - 1.0, 1.0
    )
    up_ratio = jnp.maximum(upper_n * upper_n - order_m * order_m, 0.0) / (
        4.0 * upper_n * upper_n - 1.0
    )
    real = offset < COLS
    eps_down = jnp.where((degree > order_int) & real, ROTATION * jnp.sqrt(down_ratio), 0.0)
    eps_up = jnp.where((degree + 1 < WAVES) & real, ROTATION * jnp.sqrt(up_ratio), 0.0)
    return in_first, eps_down, eps_up


def lane_group(position):
    lane = lax.broadcasted_iota(jnp.int32, (DEVS, LANES), 1)
    lane = lane - (GROUP * position) % LANES
    lane = jnp.where(lane < 0, lane + LANES, lane)
    return lane < GROUP


def unpack_columns(recv_ref, pack_scr, cycle_scr):
    pack_scr[...] = recv_ref[...].astype(F32).reshape(DEVS * SUB, LANES)
    for half in range(2):
        rows = [pack_scr[pl.ds(x * 2 + half, DEVS, stride=SUB), :] for x in range(4)]
        for c in range(HALF_CYCLES):
            merged = rows[3]
            for x in range(3):
                merged = jnp.where(lane_group(c + x), rows[x], merged)
            if c:
                merged = pltpu.roll(merged, LANES - GROUP * c, axis=1)
            cycle_scr[pl.ds(half * HALF_CYCLES + c, DEVS, stride=CYCLES), :] = merged
    return jnp.concatenate(
        [jnp.transpose(cycle_scr[t * LANES : (t + 1) * LANES, :])[:96] for t in range(NLAT // LANES)], axis=1
    )


def analyse(column, leg_ref):
    last = leg_ref[WAVES:COLS, :].astype(F32)
    spec_last = jnp.sum(column * last, axis=1, keepdims=True)
    spec = lax.dot_general(column.astype(BF16), leg_ref[:WAVES, :], NT, preferred_element_type=F32)
    first_lane = lax.broadcasted_iota(jnp.int32, (96, LANES), 1) == 0
    return spec, jnp.where(first_lane, spec_last, 0.0)


def solve(rhs, inv_ref, pole_ref, eps_down, eps_up):
    def couple(cur_real, cur_imag):
        return (
            eps_down * shift_prev(cur_real) + eps_up * shift_next(cur_real),
            eps_down * shift_prev(cur_imag) + eps_up * shift_next(cur_imag),
        )

    def apply(pole, row, terms):
        real, imag = None, None
        for c, (re, im) in terms:
            inv_re = inv_ref[pole, 0, row, c]
            inv_im = inv_ref[pole, 1, row, c]
            add_re = inv_re * re - inv_im * im
            add_im = inv_re * im + inv_im * re
            real = add_re if real is None else real + add_re
            imag = add_im if imag is None else imag + add_im
        return real, imag

    combined = [[None, None] for _ in range(FIELDS)]
    for pole in range(2):
        base = [apply(pole, f, list(enumerate(rhs))) for f in range(FIELDS)]
        div, vort = base[1], base[2]
        for step in range(ITERS):
            to_div, to_vort = couple(*vort), couple(*div)
            fields = range(FIELDS) if step == ITERS - 1 else (1, 2)
            solution = {}
            for f in fields:
                re, im = apply(pole, f, [(1, to_div), (2, to_vort)])
                solution[f] = (base[f][0] - re, base[f][1] - im)
            div, vort = solution[1], solution[2]
        beta_re = pole_ref[pole, 0]
        beta_im = pole_ref[pole, 1]
        for f in range(FIELDS):
            re, im = solution[f]
            add_re = beta_re * re - beta_im * im
            add_im = beta_re * im + beta_im * re
            combined[f][0] = add_re if pole == 0 else combined[f][0] + add_re
            combined[f][1] = add_im if pole == 0 else combined[f][1] + add_im
    return [combined[f][part] for part in range(2) for f in range(FIELDS)]


def synthesize(groups, in_even, pair, leg_ref):
    even = jnp.concatenate([jnp.where(in_even, g, 0.0) for g in groups], axis=0)
    odd = jnp.concatenate([jnp.where(in_even, 0.0, g) for g in groups], axis=0)
    both = jnp.concatenate([even, odd], axis=0).astype(BF16)
    synth = lax.dot_general(both[:, :WAVES], leg_ref[:WAVES, :], NN, preferred_element_type=F32)
    synth = synth + both[:, WAVES : WAVES + 1].astype(F32) * leg_ref[WAVES:COLS, :].astype(F32)
    row_at = lax.broadcasted_iota(jnp.int32, (96, NLAT), 0)
    return jnp.where((row_at < 48) & (pair == 0), synth, synth * 2.0)


def pack_messages(synth, send_ref, pack_scr, cycle_scr):
    synth = jnp.concatenate([synth, jnp.zeros((32, NLAT), F32)], axis=0)
    for t in range(NLAT // LANES):
        cycle_scr[t * LANES : (t + 1) * LANES, :] = jnp.transpose(synth[:, t * LANES : (t + 1) * LANES])
    for half in range(2):
        turned = []
        for c in range(HALF_CYCLES):
            values = cycle_scr[pl.ds(half * HALF_CYCLES + c, DEVS, stride=CYCLES), :]
            turned.append(pltpu.roll(values, GROUP * c, axis=1) if c else values)
        for x in range(4):
            merged = turned[HALF_CYCLES - 1]
            for c in range(HALF_CYCLES - 1):
                merged = jnp.where(lane_group(c + x), turned[c], merged)
            pack_scr[pl.ds(x * 2 + half, DEVS, stride=SUB), :] = merged
    send_ref[...] = pack_scr[...].reshape(DEVS, SUB, LANES).astype(BF16)


def middle_kernel(
    owner_ref, pair_ref, pole_ref, recv_ref, leg_hbm, inv_hbm, send_ref,
    leg_scr, inv_scr, spec_scr, pack_in, cycle_in, pack_out, cycle_out, leg_sem, inv_sem,
):
    step = pl.program_id(0)

    def leg_copy(slot):
        return pltpu.make_async_copy(leg_hbm.at[slot], leg_scr.at[slot], leg_sem.at[slot])

    def inv_copy(slot):
        return pltpu.make_async_copy(inv_hbm.at[slot], inv_scr.at[slot], inv_sem.at[slot])

    def store_spec(spec, spec_last):
        spec_scr[:, :WAVES] = spec
        spec_scr[:, WAVES:] = spec_last

    def right_side(slot):
        pair = pair_ref[owner_ref[0] * SLOTS + slot]
        in_first, eps_down, eps_up = coupling_weights(pair)
        in_even = in_first == ((pair & 1) == 0)
        rhs = [
            jnp.where(in_even, spec_scr[g * MODES : (g + 1) * MODES, :], spec_scr[48 + g * MODES : 56 + g * MODES, :])
            for g in range(6)
        ]
        return pair, in_even, [(rhs[f], rhs[3 + f]) for f in range(FIELDS)], eps_down, eps_up

    @pl.when(step == 0)
    def _():
        leg_copy(0).start()
        inv_copy(0).start()
        leg_copy(1).start()
        column = unpack_columns(recv_ref, pack_in, cycle_in)
        leg_copy(0).wait()
        inv_copy(1).start()
        leg_copy(2).start()
        store_spec(*analyse(column, leg_scr.at[0]))

    @pl.when((step > 0) & (step < SLOTS))
    def _():
        inv_copy(step - 1).wait()
        leg_copy(step).wait()

        @pl.when(step + 1 < SLOTS)
        def _():
            inv_copy(step + 1).start()

        @pl.when(step + 2 < SLOTS)
        def _():
            leg_copy(step + 2).start()

        pair, in_even, rhs, eps_down, eps_up = right_side(step - 1)
        column = unpack_columns(recv_ref, pack_in, cycle_in)
        spec = analyse(column, leg_scr.at[step])
        groups = solve(rhs, inv_scr.at[step - 1], pole_ref, eps_down, eps_up)
        store_spec(*spec)
        synth = synthesize(groups, in_even, pair, leg_scr.at[step - 1])
        pack_messages(synth, send_ref, pack_out, cycle_out)

    @pl.when(step == SLOTS)
    def _():
        inv_copy(SLOTS - 1).wait()
        pair, in_even, rhs, eps_down, eps_up = right_side(SLOTS - 1)
        groups = solve(rhs, inv_scr.at[SLOTS - 1], pole_ref, eps_down, eps_up)
        synth = synthesize(groups, in_even, pair, leg_scr.at[SLOTS - 1])
        pack_messages(synth, send_ref, pack_out, cycle_out)


def backward_kernel(recv_ref, table_ref, out_hbm, pack_scr, wave_scr, out_scr, out_sem):
    step = pl.program_id(0)
    width = table_ref.shape[-1]

    @pl.when(step == 0)
    def _():
        pack_scr[...] = recv_ref[...].astype(F32).reshape(DEVS * ROWS, LANES)
        for slot in range(SLOTS):
            for x in range(4):
                parity, part = x // 2, x % 2
                at = (slot * 2 + part) * LANES
                for half in range(2):
                    row = slot * SUB + x * 2 + half
                    turned = jnp.transpose(pack_scr[pl.ds(row, DEVS, stride=ROWS), :])
                    if x:
                        turned = jnp.concatenate([turned[GROUP * x :], turned[: GROUP * x]], axis=0)
                    wave_scr[parity, half * LANES : (half + 1) * LANES, at : at + LANES] = turned.astype(BF16)

    even = lax.dot_general(wave_scr[0], table_ref[0], NN, preferred_element_type=F32)
    odd = lax.dot_general(wave_scr[1], table_ref[1], NN, preferred_element_type=F32)
    near = even + odd
    far = even - odd
    slot = step % 2

    def leave(when):
        at = pl.multiple_of(when * width, width)
        return [
            pltpu.make_async_copy(
                out_scr.at[when % 2, side],
                out_hbm.at[:, :, :, pl.ds(side * HALF + at, width)],
                out_sem.at[when % 2, side],
            )
            for side in range(2)
        ]

    @pl.when(step >= 2)
    def _():
        for copy in leave(step - 2):
            copy.wait()

    for half in range(2):
        for c in range(HALF_CYCLES):
            for field in range(FIELDS):
                row = half * LANES + (c * FIELDS + field) * MODES
                cycle = half * HALF_CYCLES + c
                out_scr[slot, 0, field, cycle, :, :] = near[row : row + MODES]
                out_scr[slot, 1, field, cycle, :, :] = far[row : row + MODES]

    for copy in leave(step):
        copy.start()

    @pl.when(step == pl.num_programs(0) - 1)
    def _():
        for when in (step - 1, step):
            for copy in leave(when):
                copy.wait()


def whole(shape):
    return pl.BlockSpec(shape, lambda i: (0,) * len(shape))


def exchange(messages):
    return lax.all_to_all(messages, AXES, split_axis=0, concat_axis=0, tiled=True)


def on_device(fields, cycle_weights, legendre, inverses, pole_coeffs, pair_order):
    owner = lax.axis_index(AXES).astype(jnp.int32).reshape(1)
    smem = pl.BlockSpec(memory_space=pltpu.SMEM)
    grid_fields = jnp.transpose(fields, (1, 2, 0, 3))

    table, outgoing = pl.pallas_call(
        forward_kernel,
        grid=(SLOTS,),
        in_specs=[
            smem,
            whole((SLOTS, LANES)),
            whole((FIELDS, CYCLES, MODES, LONS)),
        ],
        out_specs=[
            pl.BlockSpec((2, 2 * DEVS, HALF), lambda i: (0, i, 0)),
            pl.BlockSpec((DEVS, SUB, LANES), lambda i: (0, i, 0)),
        ],
        out_shape=[
            jax.ShapeDtypeStruct((2, HALF, HALF), BF16),
            jax.ShapeDtypeStruct((DEVS, ROWS, LANES), BF16),
        ],
        scratch_shapes=[
            pltpu.VMEM((2, 256, HALF), BF16),
            pltpu.VMEM((DEVS * SUB, LANES), F32),
        ],
        name="forward",
    )(cycle_weights, pair_order.reshape(SLOTS, LANES), grid_fields)

    incoming = exchange(outgoing)

    leg = jnp.transpose(legendre, (1, 2, 0))
    inv = jnp.transpose(inverses, (2, 0, 3, 4, 5, 1, 6))
    inv = jnp.pad(inv, ((0, 0),) * 6 + ((0, WIDE - COLS),))

    anywhere = pl.BlockSpec(memory_space=pl.ANY)
    returning = pl.pallas_call(
        middle_kernel,
        grid=(SLOTS + 1,),
        in_specs=[
            smem,
            smem,
            smem,
            pl.BlockSpec((DEVS, SUB, LANES), lambda i: (0, jnp.minimum(i, SLOTS - 1), 0)),
            anywhere,
            anywhere,
        ],
        out_specs=pl.BlockSpec((DEVS, SUB, LANES), lambda i: (0, jnp.maximum(i - 1, 0), 0)),
        out_shape=jax.ShapeDtypeStruct((DEVS, ROWS, LANES), BF16),
        scratch_shapes=[
            pltpu.VMEM((SLOTS, COLS, NLAT), BF16),
            pltpu.VMEM((SLOTS, 2, 2, 3, 3, MODES, WIDE), F32),
            pltpu.VMEM((96, WIDE), F32),
            pltpu.VMEM((DEVS * SUB, LANES), F32),
            pltpu.VMEM((NLAT, LANES), F32),
            pltpu.VMEM((DEVS * SUB, LANES), F32),
            pltpu.VMEM((NLAT, LANES), F32),
            pltpu.SemaphoreType.DMA((SLOTS,)),
            pltpu.SemaphoreType.DMA((SLOTS,)),
        ],
        compiler_params=pltpu.CompilerParams(vmem_limit_bytes=50 << 20),
        name="middle",
    )(owner, pair_order, pole_coeffs, incoming, leg, inv)

    back = exchange(returning)

    width = 256
    result = pl.pallas_call(
        backward_kernel,
        grid=(HALF // width,),
        in_specs=[
            whole((DEVS, ROWS, LANES)),
            pl.BlockSpec((2, HALF, width), lambda i: (0, 0, i)),
        ],
        out_specs=anywhere,
        out_shape=jax.ShapeDtypeStruct((FIELDS, CYCLES, MODES, LONS), F32),
        scratch_shapes=[
            pltpu.VMEM((DEVS * ROWS, LANES), F32),
            pltpu.VMEM((2, 256, HALF), BF16),
            pltpu.VMEM((2, 2, FIELDS, CYCLES, MODES, width), F32),
            pltpu.SemaphoreType.DMA((2, 2)),
        ],
        compiler_params=pltpu.CompilerParams(vmem_limit_bytes=20 << 20),
        name="backward",
    )(back, table)
    return jnp.transpose(result, (2, 0, 1, 3))


def solution(mesh):
    return jax.shard_map(
        on_device,
        mesh=mesh,
        in_specs=(
            P(None, None, AXES, None),
            P(AXES),
            P(None, AXES, None),
            P(None, None, AXES, None, None, None, None),
            P(),
            P(),
        ),
        out_specs=P(None, None, AXES, None),
        check_vma=False,
    )
```
